256 devices in a mesh: ctx: 64 (over y_lo, z, x), wt: 4 (over y_hi, core).
Axes of the slice: x: 4, y: 4 (y_hi: 2, y_lo: 2; y = y_hi * 2 + y_lo), z: 8, core: 2. Of those that a mesh axis runs over, the one named last changes fastest.
Arguments:
- tokens: bfloat16 [32768, 4096], P('ctx'), may hold values from -6 to 6
- round_var: float32 [4096, 4096], P('ctx', 'wt'), may hold values from -6 to 6
- grid_base: bfloat16 [4096, 4096], P('ctx', 'wt'), may hold values from -8 to 7, as said below
- col_scale: float32 [4096], P('wt'), may hold values from 0.0015 to 0.006
- queries: bfloat16 [32768, 4096], P('ctx', 'wt'), may hold values from -4 to 4
- keys: bfloat16 [32768, 4096], P('ctx', 'wt'), may hold values from -4 to 4
- gates: bfloat16 [32768, 4096], P('ctx', 'wt'), may hold values from -6 to 6
- target: bfloat16 [32768, 4096], P('ctx', 'wt'), may hold values from -6 to 6
- decay_code: int32 [32], P('wt'), may hold values from 7 to 19
- boundary: int32 [128], P('ctx'), may hold values from 0 to 1, as said below
Outputs:
- gated_out: bfloat16 [32768, 4096], P('ctx', 'wt')
- rounding_grad: float32 [4096, 4096], P('ctx', 'wt')
The draws below stay inside these ranges and needn't reach their ends.
Inputs may be any that keep to these rules, and one draw needn't show every extreme that they name: `grid_base`: integer grid levels. At least one group begins after a segment boundary.
All inputs are finite; a program needn't handle non-finite values.
Results may differ from the reference program's by a relative error of at most 0.011.
Values may be sent and summed in bfloat16 or wider, within the bound.
A program may use at most 128 MiB of HBM per device.

```python
import math
import jax
import jax.numpy as jnp
from jax import lax

D = 4096
HEADS = 32
HEAD = 128
GROUP = 256
TOKENS = 32768
NCH = 128


def draw_grid_base(key, part):
    level = jnp.floor(jax.random.normal(key, (D, HEADS * HEAD), jnp.float32) * 3.0)
    return jnp.clip(level, -8.0, 7.0).astype(jnp.bfloat16)


def draw_boundary(key, part):
    scattered_key = jax.random.fold_in(key, 11)
    forced_key = jax.random.fold_in(key, 23)
    scattered = jax.random.randint(scattered_key, (NCH,), 0, NCH) == 0
    forced_at = jax.random.randint(forced_key, (), 0, NCH)
    forced = jnp.arange(NCH) == forced_at
    return (scattered | forced).astype(jnp.int32)


def touch_ends(drawn, stream_key, low, top_value):
    dims = drawn.shape
    spot = [jax.random.randint(jax.random.fold_in(stream_key, axis), (), 0, dims[axis]) for axis in range(len(dims))]
    drawn = drawn.at[tuple(spot)].set(low)
    longest = dims.index(max(dims))
    spot[longest] = (spot[longest] + 1) % dims[longest]
    return drawn.at[tuple(spot)].set(top_value)


def levels(own_key, shape, split, low, high):
    def one(dim, parts):
        heights = jax.random.uniform(jax.random.fold_in(jax.random.fold_in(own_key, 6), dim), (parts,), jnp.float32, low / len(split), high / len(split))
        return jnp.repeat(jnp.exp(heights), shape[dim] // parts).reshape((-1,) + (1,) * (len(shape) - dim - 1))

    factor_of = one(*split[0])
    for cut in split[1:]:
        factor_of = factor_of * one(*cut)
    return factor_of


def scatter_about(own_key, shape, scale, most, split=(), dtype=jnp.bfloat16):
    entries = scale * jax.random.normal(own_key, shape, jnp.float32)
    if split:
        entries = entries * levels(own_key, shape, split, -0.22, 0.18)
    return jnp.clip(entries, -most, most).astype(dtype)


def setup_inputs(seed: int = 0) -> dict:
    seeds = jax.random.split(jax.random.key(seed), 11)
    tokens = scatter_about(seeds[0], (TOKENS, D), 1.0, 6.0, ((0, 64),))
    round_var = scatter_about(seeds[1], (D, HEADS * HEAD), 2.0, 6.0, ((0, 64), (1, 4)), jnp.float32)
    grid_base = draw_grid_base(jax.random.fold_in(seeds[10], 71), 0)
    col_scale = jnp.clip(jnp.exp(math.log(0.006) - 1.3862944 * jax.random.uniform(seeds[3], (HEADS * HEAD,), jnp.float32) ** levels(seeds[3], (HEADS * HEAD,), ((0, 4),), -0.2, 0.2)), 0.0015, 0.006)
    queries = scatter_about(seeds[4], (TOKENS, HEADS * HEAD), 0.3, 4.0, ((0, 64), (1, 4)))
    keys = scatter_about(seeds[5], (TOKENS, HEADS * HEAD), 0.3, 4.0, ((0, 64), (1, 4)))
    gates = scatter_about(seeds[6], (TOKENS, HEADS * HEAD), 1.0, 6.0, ((0, 64), (1, 4)))
    target = scatter_about(seeds[7], (TOKENS, HEADS * HEAD), 1.0, 6.0, ((0, 64), (1, 4)))
    decay_code = touch_ends(jax.random.randint(seeds[8], (HEADS,), 7, 20), jax.random.fold_in(seeds[8], 1), 7, 19).astype(jnp.int32)
    boundary = draw_boundary(jax.random.fold_in(seeds[10], 71), 0)
    return {"tokens": tokens, "round_var": round_var, "grid_base": grid_base, "col_scale": col_scale, "queries": queries, "keys": keys, "gates": gates, "target": target, "decay_code": decay_code, "boundary": boundary}


epsilon = 1e-06
loss_weight = 1024.0

def tables(decay_code):
    decay_rate = jnp.exp2(-decay_code.astype(jnp.float32))
    offsets = jnp.arange(GROUP).astype(jnp.float32)
    query_decay = jnp.exp(-offsets[:, None] * decay_rate[None, :])
    key_decay = jnp.exp(-(GROUP - offsets)[:, None] * decay_rate[None, :])
    spacing = offsets[:, None] - offsets[None, :]
    causal_decay = jnp.where(spacing[None] >= 0.0, jnp.exp(-jnp.maximum(spacing, 0.0)[None] * decay_rate[:, None, None]), 0.0)
    group_decay = jnp.exp(-GROUP * decay_rate)
    return (query_decay, key_decay, causal_decay, group_decay)

def group_parts(query_rows, key_rows, query_decay, key_decay, causal_decay):
    scores = jnp.einsum('ihd,jhd->hij', query_rows.astype(jnp.float32), key_rows.astype(jnp.float32))
    weights = (scores * causal_decay).astype(jnp.bfloat16)
    query_dec = (query_rows.astype(jnp.float32) * query_decay[:, :, None]).astype(jnp.bfloat16)
    key_dec = (key_rows.astype(jnp.float32) * key_decay[:, :, None]).astype(jnp.bfloat16)
    return (weights, query_dec, key_dec)

def reference(tokens, round_var, grid_base, col_scale, queries, keys, gates, target, decay_code, boundary):
    squash = jax.nn.sigmoid(round_var)
    raw_level = 1.2 * squash - 0.1
    soft_part = jnp.clip(raw_level, 0.0, 1.0)
    slopes = jnp.where((raw_level > 0.0) & (raw_level < 1.0), 1.2 * squash * (1.0 - squash), 0.0)
    weight = (col_scale[None, :] * (grid_base.astype(jnp.float32) + soft_part)).astype(jnp.bfloat16)
    values = jnp.dot(tokens, weight, preferred_element_type=jnp.float32).astype(jnp.bfloat16)
    query_decay, key_decay, causal_decay, group_decay = tables(decay_code)
    shape4 = (NCH, GROUP, HEADS, HEAD)
    query_all = queries.reshape(shape4)
    key_all = keys.reshape(shape4)
    value_all = values.reshape(shape4)
    multiplier = 1.0 - 0.5 * boundary.astype(jnp.float32)

    def forward_turn(pending, group_in):
        query_rows, key_rows, value_rows, factor = group_in
        weights, query_dec, key_dec = group_parts(query_rows, key_rows, query_decay, key_decay, causal_decay)
        state = factor * pending
        intra = jnp.einsum('hij,jhe->ihe', weights.astype(jnp.float32), value_rows.astype(jnp.float32))
        inter = jnp.einsum('ihd,hde->ihe', query_dec.astype(jnp.float32), state.astype(jnp.bfloat16).astype(jnp.float32))
        update = jnp.einsum('jhd,jhe->hde', key_dec.astype(jnp.float32), value_rows.astype(jnp.float32))
        return (group_decay[:, None, None] * state + update, intra + inter)
    start_state = jnp.zeros((HEADS, HEAD, HEAD), jnp.float32)
    _, attn_all = lax.scan(forward_turn, start_state, (query_all, key_all, value_all, multiplier))
    attn = attn_all.reshape(TOKENS, HEADS * HEAD)
    rms = jnp.sqrt(lax.optimization_barrier(jnp.sum(attn * attn, axis=1)) / (HEADS * HEAD) + epsilon)
    normed = attn / rms[:, None]
    gate_open = jax.nn.sigmoid(gates.astype(jnp.float32))
    gated = normed * gate_open
    gated_out = gated.astype(jnp.bfloat16)
    grad_gated = (gated - target.astype(jnp.float32)) * (loss_weight / math.sqrt(TOKENS))
    grad_normed = grad_gated * gate_open
    inner = lax.optimization_barrier(jnp.sum(grad_normed * normed, axis=1)) / (HEADS * HEAD)
    grad_attn = ((grad_normed - normed * inner[:, None]) / rms[:, None]).astype(jnp.bfloat16)
    grad_all = grad_attn.reshape(shape4)

    def backward_turn(later_state, group_in):
        query_rows, key_rows, grad_rows, factor = group_in
        weights, query_dec, key_dec = group_parts(query_rows, key_rows, query_decay, key_decay, causal_decay)
        intra = jnp.einsum('hij,ihe->jhe', weights.astype(jnp.float32), grad_rows.astype(jnp.float32))
        inter = jnp.einsum('jhd,hde->jhe', key_dec.astype(jnp.float32), later_state.astype(jnp.bfloat16).astype(jnp.float32))
        collected = jnp.einsum('ihd,ihe->hde', query_dec.astype(jnp.float32), grad_rows.astype(jnp.float32))
        new_state = factor * (collected + group_decay[:, None, None] * later_state)
        return (new_state, (intra + inter).astype(jnp.bfloat16))
    _, grad_values = lax.scan(backward_turn, start_state, (query_all, key_all, grad_all, multiplier), reverse=True)
    grad_values = grad_values.reshape(TOKENS, HEADS * HEAD)
    weight_grad = jnp.dot(tokens.T, grad_values, preferred_element_type=jnp.float32)
    rounding_grad = col_scale[None, :] * slopes * weight_grad
    return (gated_out, rounding_grad)
```

```python
import functools, heapq, math
import jax
import jax.numpy as jnp
from jax import lax
from jax.sharding import PartitionSpec as P
from jax.experimental import pallas as pl
from jax.experimental.pallas import tpu as pltpu

MESH = pl.DeviceIdType.MESH
NX, NZ, NY = 4, 8, 2
SPLIT = 384
BF = jnp.bfloat16
F32 = jnp.float32


def place():
    ctx = lax.axis_index("ctx")
    wt = lax.axis_index("wt")
    x = lax.rem(ctx, NX)
    z = lax.rem(lax.div(ctx, NX), NZ)
    y = lax.div(ctx, NX * NZ)
    return x, y, z, wt


def at(x, y, z, wt):
    return (y * (NX * NZ) + z * NX + x, wt)


def meet(peers):
    barrier = pltpu.get_barrier_semaphore()
    for peer in peers:
        pl.semaphore_signal(barrier, inc=1, device_id=peer, device_id_type=MESH)
    pl.semaphore_wait(barrier, len(peers))


def scan_kernel(reverse, part_ref, rate_ref, out_ref, xbuf, pref, tbuf, ybuf, zbuf, rbuf, obuf,
                s1, r1, s2, r2, s3, r3, s4, r4):
    x, y, z, wt = place()
    j = y * NZ + z
    rows = [lax.rem(x + k, NX) for k in range(1, NX)]
    cols = [lax.rem(j + k, NY * NZ) for k in range(1, NY * NZ)]
    row_dev = [at(p, y, z, wt) for p in rows]
    col_dev = [at(x, lax.div(p, NZ), lax.rem(p, NZ), wt) for p in cols]
    meet(row_dev + col_dev)

    def go(src, dst, ssem, rsem, dev):
        c = pltpu.make_async_remote_copy(
            src_ref=src, dst_ref=dst, send_sem=ssem, recv_sem=rsem, device_id=dev, device_id_type=MESH
        )
        c.start()
        return c

    one = [
        go(part_ref.at[p], xbuf.at[x], s1.at[k], r1.at[k], d)
        for k, (p, d) in enumerate(zip(rows, row_dev))
    ]
    xbuf[x] = part_ref[x]
    rate = rate_ref[pl.ds(x * 16, 16)]
    rate1 = rate_ref[x * 16 + j]
    rate4 = (rate1 * rate1) * (rate1 * rate1)
    for c in one:
        c.wait_recv()
    order = list(reversed(range(NX))) if reverse else list(range(NX))
    total = jnp.zeros((16, 16, 128), F32)
    mult = jnp.ones((16, 128), F32)
    mults = []
    for i in order:
        pref[i] = total
        mults.append(mult)
        m = xbuf[i, 16].astype(F32)
        total = (rate * m[None]) * total + xbuf[i, pl.ds(0, 16)].astype(F32)
        mult = mult * m
    tbuf[:, 0] = total.astype(BF)
    tbuf[:, 1] = jnp.broadcast_to(mult.astype(BF)[None], (16, 16, 128))
    two = [
        go(tbuf.at[p], ybuf.at[j], s2.at[k], r2.at[k], d)
        for k, (p, d) in enumerate(zip(cols, col_dev))
    ]
    ybuf[j] = tbuf[j]
    for c in two:
        c.wait_recv()
    state = jnp.zeros((16, 128), F32)
    span = NY * NZ
    for i in (reversed(range(span)) if reverse else range(span)):
        zbuf[i] = state.astype(BF)
        state = (rate4 * ybuf[i, 1].astype(F32)) * state + ybuf[i, 0].astype(F32)
    three = [
        go(zbuf.at[p], rbuf.at[j], s3.at[k], r3.at[k], d)
        for k, (p, d) in enumerate(zip(cols, col_dev))
    ]
    rbuf[j] = zbuf[j]
    for c in three:
        c.wait_recv()
    entering = rbuf[...].astype(F32)
    grow = jnp.ones((16, 1, 128), F32)
    for n, i in enumerate(order):
        obuf[i] = (pref[i] + (grow * mults[n][None]) * entering).astype(BF)
        grow = grow * rate
    four = [
        go(obuf.at[p], out_ref.at[x], s4.at[k], r4.at[k], d)
        for k, (p, d) in enumerate(zip(rows, row_dev))
    ]
    out_ref[x] = obuf[x]
    for c in four:
        c.wait_recv()
    for c in one + two + three + four:
        c.wait_send()


def scan_states(part, mult, rate2, reverse):
    quarters = part.astype(BF).reshape(NX, 16, 16, 128)
    tile = jnp.broadcast_to(mult.astype(BF), (NX, 1, 16, 128))
    packed = jnp.concatenate([quarters, tile], axis=1)
    rates = jnp.broadcast_to(rate2[:, None, None, None], (8, 8, 1, 128)).reshape(64, 1, 128)
    vm = pl.BlockSpec(memory_space=pltpu.VMEM)
    out = pl.pallas_call(
        functools.partial(scan_kernel, reverse),
        out_shape=jax.ShapeDtypeStruct((NX, 16, 16, 128), BF),
        in_specs=[vm, vm],
        out_specs=vm,
        scratch_shapes=[
            pltpu.VMEM((NX, 17, 16, 128), BF),
            pltpu.VMEM((NX, 16, 16, 128), F32),
            pltpu.VMEM((16, 2, 16, 128), BF),
            pltpu.VMEM((16, 2, 16, 128), BF),
            pltpu.VMEM((16, 16, 128), BF),
            pltpu.VMEM((16, 16, 128), BF),
            pltpu.VMEM((NX, 16, 16, 128), BF),
        ]
        + [pltpu.SemaphoreType.DMA((n,)) for n in (3, 3, 15, 15, 15, 15, 3, 3)],
        compiler_params=pltpu.CompilerParams(collective_id=2 if reverse else 1, has_side_effects=True),
        name="state_scan_back" if reverse else "state_scan",
    )(packed, rates)
    return out.reshape(8, 128, 128)


LAT = 1.7
RATE = 90e3 / 2


class Links:
    def __init__(self):
        self.free = {}

    def send(self, link, now, nbytes):
        start = max(now, self.free.get(link, 0.0))
        done = start + nbytes / RATE
        self.free[link] = done
        return done + LAT


def gather_plan():
    width = {0: SPLIT, 1: 1024 - SPLIT}
    links = Links()
    heap = []
    plan = []
    seq = [0]
    have = {}

    def push(link, now, key, halves):
        color, oz, ox, _ = key
        nbytes = halves * 64 * width[color] * 2
        seq[0] += 1
        heapq.heappush(heap, (links.send(link, now, nbytes), seq[0], link, key))
        return seq[0] - 1

    def sends_for(color, link, oz, ox):
        out = []
        axis = link[0]
        first, second = ("x", "z") if color == 0 else ("z", "x")
        size = {"x": NX, "z": NZ}
        off = {"x": ox, "z": oz}
        if axis in "xz":
            dist = abs(off[axis])
            if dist < size[axis] // 2:
                out.append((link, 0 if link[1] == "+" else 1) if dist == size[axis] // 2 - 1 else (link, None))
        if axis == "y":
            out += [(first + "+", None), (first + "-", None)]
        if axis in ("y", first):
            out += [(second + "+", None), (second + "-", None)]
        return out

    def emit(now, color, link, oz, ox, skip_second=False):
        for nxt, half in sends_for(color, link, oz, ox):
            if skip_second and nxt[0] != link[0]:
                continue
            step = 1 if nxt[1] == "+" else -1
            n_oz = oz - step if nxt[0] == "z" else oz
            n_ox = ox - step if nxt[0] == "x" else ox
            sid = push(nxt, now, (color, n_oz, n_ox, half), 1 if half is not None else 2)
            plan.append(("send", sid, color, nxt, oz, ox, half))

    for color in (1, 0):
        sid = push("y", 0.0, (color, 0, 0, None), 1)
        plan.append(("send", sid, color, "y", 0, 0, None))
    count = {}
    parts = {}
    while heap:
        now, sq, link, key = heapq.heappop(heap)
        color, oz, ox, half = key
        first = "x" if color == 0 else "z"
        plan.append(("recv", sq - 1))
        size = {"x": NX, "z": NZ, "y": 2}[link[0]]
        whole = True
        if half is not None:
            spot = (color, oz % NZ, ox % NX)
            parts[spot] = parts.get(spot, 0) + 1
            whole = parts[spot] == 2
            if whole and link[0] == first:
                second = "z" if color == 0 else "x"
                for sign in "+-":
                    step = 1 if sign == "+" else -1
                    n_oz = oz - step if second == "z" else oz
                    n_ox = ox - step if second == "x" else ox
                    sid = push(second + sign, now, (color, n_oz, n_ox, None), 2)
                    plan.append(("send", sid, color, second + sign, oz, ox, None))
        else:
            emit(now, color, link, oz, ox)
        if whole:
            spot = (color, oz % NZ)
            count[spot] = count.get(spot, 0) + 1
            if count[spot] == NX:
                plan.append(("product", color, oz % NZ))
    return plan, seq[0], max(links.free.values())


def gather_kernel(plan, tok_ref, w_ref, out_ref, wa, wb, acc, ssem, rsem):
    x, y, z, wt = place()
    peers = {
        "x+": at(lax.rem(x + 1, NX), y, z, wt),
        "x-": at(lax.rem(x + NX - 1, NX), y, z, wt),
        "z+": at(x, y, lax.rem(z + 1, NZ), wt),
        "z-": at(x, y, lax.rem(z + NZ - 1, NZ), wt),
        "y": at(x, 1 - y, z, wt),
    }
    meet(list(peers.values()))
    buf = (wa, wb)
    lanes = ((0, SPLIT), (SPLIT, 1024))
    copies = {}
    for op in plan:
        if op[0] == "send":
            _, sid, color, link, oz, ox, half = op
            w = buf[color]
            if link == "y":
                lo, hi = lanes[color]
                src = w_ref.at[:, lo:hi]
                dst = w.at[y, z, x]
            else:
                zz = lax.rem(z + (oz + 2 * NZ), NZ)
                xx = lax.rem(x + (ox + 2 * NX), NX)
                dst = w.at[:, zz, xx] if half is None else w.at[half, zz, xx]
                src = dst
            c = pltpu.make_async_remote_copy(
                src_ref=src, dst_ref=dst, send_sem=ssem.at[sid], recv_sem=rsem.at[sid],
                device_id=peers[link], device_id_type=MESH,
            )
            c.start()
            copies[sid] = c
            if len(copies) == 2:
                wa[y, z, x] = w_ref[:, :SPLIT]
                wb[y, z, x] = w_ref[:, SPLIT:]
                acc[...] = jnp.zeros_like(acc)
        elif op[0] == "recv":
            copies[op[1]].wait_recv()
        else:
            _, color, oz = op
            zz = lax.rem(z + oz, NZ)
            lo, hi = lanes[color]
            w = buf[color]

            @pl.loop(0, 4)
            def _(i, zz=zz, lo=lo, hi=hi, w=w):
                r = pl.ds(pl.multiple_of(i * 128, 128), 128)
                t0 = tok_ref[r, pl.ds(pl.multiple_of(zz * 256, 256), 256)]
                t1 = tok_ref[r, pl.ds(pl.multiple_of(zz * 256 + 2048, 256), 256)]
                acc[r, lo:hi] += jnp.dot(
                    t0, w[0, zz].reshape(256, hi - lo), preferred_element_type=F32
                ) + jnp.dot(t1, w[1, zz].reshape(256, hi - lo), preferred_element_type=F32)
    out_ref[...] = acc[...].astype(BF)
    for c in copies.values():
        c.wait_send()


def project(tokens, weight):
    plan, n, _ = gather_plan()
    vm = pl.BlockSpec(memory_space=pltpu.VMEM)
    return pl.pallas_call(
        functools.partial(gather_kernel, plan),
        out_shape=jax.ShapeDtypeStruct((512, 1024), BF),
        in_specs=[vm, vm],
        out_specs=vm,
        scratch_shapes=[
            pltpu.VMEM((NY, NZ, NX, 64, SPLIT), BF),
            pltpu.VMEM((NY, NZ, NX, 64, 1024 - SPLIT), BF),
            pltpu.VMEM((512, 1024), F32),
            pltpu.SemaphoreType.DMA((n,)),
            pltpu.SemaphoreType.DMA((n,)),
        ],
        compiler_params=pltpu.CompilerParams(
            collective_id=3, has_side_effects=True, vmem_limit_bytes=60 * 2**20
        ),
        name="weight_gather_product",
    )(tokens, weight)


CHUNKS = (4, 3, 5, 2, 6, 1, 7, 0)
CHUNK_US = 1.3


def ring(color, stage):
    axis = ("z", "x") if color == 0 else ("x", "z")
    return axis[stage - 1], {"x": NX, "z": NZ}[axis[stage - 1]]


def reduce_plan():
    width = {0: SPLIT, 1: 1024 - SPLIT}
    links = Links()
    needs = {}
    inst_of = {(0, 1): (2, 1, 3, 0), (1, 1): CHUNKS, (0, 2): (0,), (1, 2): (0,)}
    for color in (1, 0):
        for stage in (1, 2):
            axis, n = ring(color, stage)
            for inst in inst_of[color, stage]:
                for flow in (-1, 1):
                    for k in range(n // 2, 0, -1):
                        task = ("s", color, stage, flow, inst, k)
                        there = (flow * k) % n
                        if stage == 1:
                            dep = [("chunk", there if color == 0 else inst)]
                        else:
                            dep = [("q", color, 1, there)]
                        if k < n // 2:
                            dep.append(("got", color, stage, flow, inst, k + 1))
                        needs[task] = dep
                dep = [("got", color, stage, flow, inst, 1) for flow in (-1, 1)]
                if stage == 1:
                    dep.append(("chunk", 0 if color == 0 else inst))
                else:
                    dep.append(("q", color, 1, 0))
                needs[("q", color, stage, inst)] = dep
        needs[("y", color)] = [("q", color, 2, 0)]
        needs[("out", color)] = [("goty", color)]
    done = set()
    plan = []
    heap = []
    seq = [0]

    def post(t, event):
        seq[0] += 1
        heapq.heappush(heap, (t, seq[0], event))

    for i, oz in enumerate(CHUNKS):
        post(CHUNK_US * (i + 1), ("chunk", oz))
    sids = {}
    last = 0.0
    while heap:
        t, _, event = heapq.heappop(heap)
        last = t
        done.add(event)
        if event[0] == "chunk":
            plan.append(event)
        moved = True
        while moved:
            moved = False
            for task in list(needs):
                if all(d in done for d in needs[task]):
                    del needs[task]
                    plan.append(task)
                    moved = True
                    if task[0] == "s":
                        _, color, stage, flow, inst, k = task
                        axis, n = ring(color, stage)
                        halves = 1 if k == n // 2 else 2
                        arrive = links.send((axis, flow), t, halves * 64 * width[color] * 2)
                        post(arrive, ("got",) + task[1:])
                        sids[task] = len(sids)
                    elif task[0] == "y":
                        post(links.send("y", t, 64 * width[task[1]] * 2), ("goty", task[1]))
                        sids[task] = len(sids)
                    elif task[0] == "q":
                        done.add(task)
    return plan, sids, last


def reduce_kernel(plan, sids, tok_ref, gv_ref, factor_ref, out_ref, pa, pb, ra1, rb1, ra2, rb2,
                  qa, qb, fa, fb, ya, yb, va, vb, ssem, rsem):
    x, y, z, wt = place()
    peers = {
        ("x", 1): at(lax.rem(x + 1, NX), y, z, wt),
        ("x", -1): at(lax.rem(x + NX - 1, NX), y, z, wt),
        ("z", 1): at(x, y, lax.rem(z + 1, NZ), wt),
        ("z", -1): at(x, y, lax.rem(z + NZ - 1, NZ), wt),
        "y": at(x, 1 - y, z, wt),
    }
    meet(list(peers.values()))
    mine = (pa, pb)
    quit_ = (qa, qb)
    slots = {(0, 1): ra1, (1, 1): rb1, (0, 2): ra2, (1, 2): rb2}
    full = (fa, fb)
    ysend = (ya, yb)
    yrecv = (va, vb)
    lanes = ((0, SPLIT), (SPLIT, 1024))
    copies = {}

    def slot(color, stage, flow, inst, k):
        r = slots[color, stage]
        f = 0 if flow < 0 else 1
        return r.at[f, inst, k] if stage == 1 else r.at[f, k]

    def own(color, stage, inst, there):
        if stage == 2:
            return quit_[color].at[there]
        oz, ox = (there, inst) if color == 0 else (inst, there)
        return mine[color].at[:, lax.rem(z + oz, NZ), lax.rem(x + ox, NX)]

    for op in plan:
        if op[0] == "chunk":
            zz = lax.rem(z + op[1], NZ)

            @pl.loop(0, 4)
            def _(i, zz=zz):
                yy = lax.div(i, 2)
                h = lax.rem(i, 2)
                cols = tok_ref[:, pl.ds(pl.multiple_of(yy * 2048 + zz * 256 + h * 128, 128), 128)]
                r = lax.dot_general(
                    cols, gv_ref[...], (((0,), (0,)), ((), ())), preferred_element_type=F32
                ).astype(BF)
                for u in range(2):
                    pa[yy, zz, h * 2 + u] = r[u * 64 : u * 64 + 64, :SPLIT]
                    pb[yy, zz, h * 2 + u] = r[u * 64 : u * 64 + 64, SPLIT:]
        elif op[0] == "s":
            _, color, stage, flow, inst, k = op
            axis, n = ring(color, stage)
            half = 0 if flow < 0 else 1
            there = (flow * k) % n
            p = own(color, stage, inst, there)
            if k == n // 2:
                src = p.at[half]
                dst = slot(color, stage, flow, inst, k - 1).at[half]
            else:
                copies["s", color, stage, flow, inst, k + 1].wait_recv()
                src = slot(color, stage, flow, inst, k)
                dst = slot(color, stage, flow, inst, k - 1)
                if k == n // 2 - 1:
                    src[half] = (src[half].astype(F32) + p[half].astype(F32)).astype(BF)
                    src[1 - half] = p[1 - half]
                else:
                    src[...] = (src[...].astype(F32) + p[...].astype(F32)).astype(BF)
            sid = sids[op]
            c = pltpu.make_async_remote_copy(
                src_ref=src, dst_ref=dst, send_sem=ssem.at[sid], recv_sem=rsem.at[sid],
                device_id=peers[axis, flow], device_id_type=MESH,
            )
            c.start()
            copies[op] = c
        elif op[0] == "q":
            _, color, stage, inst = op
            for flow in (-1, 1):
                copies["s", color, stage, flow, inst, 1].wait_recv()
            low = slot(color, stage, -1, inst, 0)
            high = slot(color, stage, 1, inst, 0)
            p = own(color, stage, inst, 0)
            total = low[...].astype(F32) + high[...].astype(F32) + p[...].astype(F32)
            if stage == 1:
                quit_[color][inst] = total.astype(BF)
            else:
                full[color][...] = total
        elif op[0] == "y":
            color = op[1]
            ysend[color][...] = full[color][1 - y].astype(BF)
            sid = sids[op]
            c = pltpu.make_async_remote_copy(
                src_ref=ysend[color], dst_ref=yrecv[color], send_sem=ssem.at[sid],
                recv_sem=rsem.at[sid], device_id=peers["y"], device_id_type=MESH,
            )
            c.start()
            copies[op] = c
        else:
            color = op[1]
            copies["y", color].wait_recv()
            lo, hi = lanes[color]
            out_ref[:, lo:hi] = factor_ref[:, lo:hi] * (
                full[color][y] + yrecv[color][...].astype(F32)
            )
    for c in copies.values():
        c.wait_send()


def gradient(tokens, grad_values, factor):
    plan, sids, _ = reduce_plan()
    n = len(sids)
    a, b = SPLIT, 1024 - SPLIT
    vm = pl.BlockSpec(memory_space=pltpu.VMEM)
    return pl.pallas_call(
        functools.partial(reduce_kernel, plan, sids),
        out_shape=jax.ShapeDtypeStruct((64, 1024), F32),
        in_specs=[vm, vm, vm],
        out_specs=vm,
        scratch_shapes=[
            pltpu.VMEM((NY, NZ, NX, 64, a), BF),
            pltpu.VMEM((NY, NZ, NX, 64, b), BF),
            pltpu.VMEM((2, NX, NZ // 2, NY, 64, a), BF),
            pltpu.VMEM((2, NZ, NX // 2, NY, 64, b), BF),
            pltpu.VMEM((2, NX // 2, NY, 64, a), BF),
            pltpu.VMEM((2, NZ // 2, NY, 64, b), BF),
            pltpu.VMEM((NX, NY, 64, a), BF),
            pltpu.VMEM((NZ, NY, 64, b), BF),
            pltpu.VMEM((NY, 64, a), F32),
            pltpu.VMEM((NY, 64, b), F32),
            pltpu.VMEM((64, a), BF),
            pltpu.VMEM((64, b), BF),
            pltpu.VMEM((64, a), BF),
            pltpu.VMEM((64, b), BF),
            pltpu.SemaphoreType.DMA((n,)),
            pltpu.SemaphoreType.DMA((n,)),
        ],
        compiler_params=pltpu.CompilerParams(
            collective_id=4, has_side_effects=True, vmem_limit_bytes=60 * 2**20
        ),
        name="weight_gradient_reduce",
    )(tokens, grad_values, factor)


HEADS = 32
HEAD = 128
GROUP = 256


epsilon = 1e-06
loss_weight = 1024.0


def tables(decay_code):
    decay_rate = jnp.exp2(-decay_code.astype(jnp.float32))
    offsets = jnp.arange(GROUP).astype(jnp.float32)
    query_decay = jnp.exp(-offsets[:, None] * decay_rate[None, :])
    key_decay = jnp.exp(-(GROUP - offsets)[:, None] * decay_rate[None, :])
    spacing = offsets[:, None] - offsets[None, :]
    causal_decay = jnp.where(
        spacing[None] >= 0.0,
        jnp.exp(-jnp.maximum(spacing, 0.0)[None] * decay_rate[:, None, None]),
        0.0,
    )
    group_decay = jnp.exp(-GROUP * decay_rate)
    return (query_decay, key_decay, causal_decay, group_decay)


def on_device(
    tokens, round_var, grid_base, col_scale, queries, keys, gates, target, decay_code, boundary
):
    squash = jax.nn.sigmoid(round_var)
    raw_level = 1.2 * squash - 0.1
    soft_part = jnp.clip(raw_level, 0.0, 1.0)
    slopes = jnp.where((raw_level > 0.0) & (raw_level < 1.0), 1.2 * squash * (1.0 - squash), 0.0)
    weight = (col_scale[None, :] * (grid_base.astype(jnp.float32) + soft_part)).astype(jnp.bfloat16)
    rows_here = tokens.shape[0]
    col_count = queries.shape[1]
    head_count = col_count // HEAD
    blocks = rows_here // GROUP
    ctx_count = lax.axis_size("ctx")
    shape4 = (blocks, GROUP, head_count, HEAD)
    value_all = project(tokens, weight).reshape(shape4)
    query_all = queries.reshape(shape4)
    key_all = keys.reshape(shape4)
    query_decay, key_decay, causal_decay, group_decay = tables(decay_code)
    scores = jnp.einsum("cihd,cjhd->chij", query_all, key_all, preferred_element_type=jnp.float32)
    weights = (scores * causal_decay[None]).astype(jnp.bfloat16)
    query_dec = (query_all * query_decay[None, :, :, None]).astype(jnp.bfloat16)
    key_dec = (key_all * key_decay[None, :, :, None]).astype(jnp.bfloat16)
    intra = jnp.einsum("chij,cjhe->cihe", weights, value_all, preferred_element_type=jnp.float32)
    updates = jnp.einsum("cjhd,cjhe->chde", key_dec, value_all, preferred_element_type=jnp.float32)
    multiplier = 1.0 - 0.5 * boundary.astype(jnp.float32)
    local_state = jnp.zeros((head_count, HEAD, HEAD), jnp.float32)
    state_coef = jnp.ones((head_count,), jnp.float32)
    local_list = []
    coef_list = []
    for block in range(blocks):
        state_coef = state_coef * multiplier[block]
        local_state = multiplier[block] * local_state
        local_list.append(local_state)
        coef_list.append(state_coef)
        local_state = group_decay[:, None, None] * local_state + updates[block]
        state_coef = state_coef * group_decay
    rate2 = group_decay * group_decay
    pair = multiplier[0] * multiplier[1]
    entering = scan_states(local_state, pair, rate2, False).astype(jnp.float32)
    states = jnp.stack(
        [
            part_state + part_coef[:, None, None] * entering
            for part_state, part_coef in zip(local_list, coef_list)
        ]
    )
    attn_all = intra + jnp.einsum(
        "cihd,chde->cihe",
        query_dec,
        states.astype(jnp.bfloat16),
        preferred_element_type=jnp.float32,
    )
    attn = attn_all.reshape(rows_here, col_count)
    row_squares = lax.psum(jnp.sum(attn * attn, axis=1), "wt")
    rms = jnp.sqrt(row_squares / (HEADS * HEAD) + epsilon)
    normed = attn / rms[:, None]
    gate_open = jax.nn.sigmoid(gates.astype(jnp.float32))
    gated = normed * gate_open
    gated_out = gated.astype(jnp.bfloat16)
    grad_gated = (gated - target.astype(jnp.float32)) * (
        loss_weight / math.sqrt(rows_here * ctx_count)
    )
    grad_normed = grad_gated * gate_open
    row_inner = lax.psum(jnp.sum(grad_normed * normed, axis=1), "wt")
    grad_attn = (
        (grad_normed - normed * (row_inner / (HEADS * HEAD))[:, None]) / rms[:, None]
    ).astype(jnp.bfloat16)
    grad_all = grad_attn.reshape(shape4)
    back_intra = jnp.einsum(
        "chij,cihe->cjhe", weights, grad_all, preferred_element_type=jnp.float32
    )
    collected = jnp.einsum(
        "cihd,cihe->chde", query_dec, grad_all, preferred_element_type=jnp.float32
    )
    later_local = jnp.zeros((head_count, HEAD, HEAD), jnp.float32)
    later_coef = jnp.ones((head_count,), jnp.float32)
    next_list = [None] * blocks
    next_coefs = [None] * blocks
    for block in reversed(range(blocks)):
        next_list[block] = later_local
        next_coefs[block] = later_coef
        later_local = multiplier[block] * (
            collected[block] + group_decay[:, None, None] * later_local
        )
        later_coef = later_coef * group_decay * multiplier[block]
    from_later = scan_states(later_local, pair, rate2, True).astype(jnp.float32)
    next_states = jnp.stack(
        [
            part_state + part_coef[:, None, None] * from_later
            for part_state, part_coef in zip(next_list, next_coefs)
        ]
    )
    grad_values = back_intra + jnp.einsum(
        "cjhd,chde->cjhe",
        key_dec,
        next_states.astype(jnp.bfloat16),
        preferred_element_type=jnp.float32,
    )
    grad_values = grad_values.astype(jnp.bfloat16).reshape(rows_here, col_count)
    rounding_grad = gradient(tokens, grad_values, col_scale[None, :] * slopes)
    return (gated_out, rounding_grad)


def solution(mesh):
    placed = (
        P("ctx", None),
        P("ctx", "wt"),
        P("ctx", "wt"),
        P("wt"),
        P("ctx", "wt"),
        P("ctx", "wt"),
        P("ctx", "wt"),
        P("ctx", "wt"),
        P("wt"),
        P("ctx"),
    )
    return jax.shard_map(
        on_device,
        mesh=mesh,
        in_specs=placed,
        out_specs=(P("ctx", "wt"), P("ctx", "wt")),
        check_vma=False,
    )
```

```python
import functools, heapq, math
import jax
import jax.numpy as jnp
from jax import lax
from jax.sharding import PartitionSpec as P
from jax.experimental import pallas as pl
from jax.experimental.pallas import tpu as pltpu

MESH = pl.DeviceIdType.MESH
NX, NZ, NY = 4, 8, 2
SPLIT = 384
HEADS = 32
HEAD = 128
GROUP = 256
LANES = ((0, SPLIT), (SPLIT, 1024))
epsilon = 1e-06
loss_weight = 1024.0
BF = jnp.bfloat16
F32 = jnp.float32


def place():
    ctx = lax.axis_index("ctx")
    wt = lax.axis_index("wt")
    x = lax.rem(ctx, NX)
    z = lax.rem(lax.div(ctx, NX), NZ)
    y = lax.div(ctx, NX * NZ)
    return x, y, z, wt


def at(x, y, z, wt):
    return (y * (NX * NZ) + z * NX + x, wt)


LAT = 1.7
RATE = 90e3 / 2


class Links:
    def __init__(self):
        self.free = {}

    def send(self, link, now, nbytes):
        start = max(now, self.free.get(link, 0.0))
        done = start + nbytes / RATE
        self.free[link] = done
        return done + LAT


def gather_plan():
    width = {0: SPLIT, 1: 1024 - SPLIT}
    links = Links()
    heap = []
    plan = []
    seq = [0]
    have = {}

    def push(link, now, key, halves):
        color, oz, ox, _ = key
        nbytes = halves * 64 * width[color] * 2
        seq[0] += 1
        heapq.heappush(heap, (links.send(link, now, nbytes), seq[0], link, key))
        return seq[0] - 1

    def sends_for(color, link, oz, ox):
        out = []
        axis = link[0]
        first, second = ("x", "z") if color == 0 else ("z", "x")
        size = {"x": NX, "z": NZ}
        off = {"x": ox, "z": oz}
        if axis in "xz":
            dist = abs(off[axis])
            if dist < size[axis] // 2:
                out.append((link, 0 if link[1] == "+" else 1) if dist == size[axis] // 2 - 1 else (link, None))
        if axis == "y":
            out += [(first + "+", None), (first + "-", None)]
        if axis in ("y", first):
            out += [(second + "+", None), (second + "-", None)]
        return out

    def emit(now, color, link, oz, ox, skip_second=False):
        for nxt, half in sends_for(color, link, oz, ox):
            if skip_second and nxt[0] != link[0]:
                continue
            step = 1 if nxt[1] == "+" else -1
            n_oz = oz - step if nxt[0] == "z" else oz
            n_ox = ox - step if nxt[0] == "x" else ox
            sid = push(nxt, now, (color, n_oz, n_ox, half), 1 if half is not None else 2)
            plan.append(("send", sid, color, nxt, oz, ox, half))

    for color in (1, 0):
        sid = push("y", 0.0, (color, 0, 0, None), 1)
        plan.append(("send", sid, color, "y", 0, 0, None))
    count = {}
    parts = {}
    while heap:
        now, sq, link, key = heapq.heappop(heap)
        color, oz, ox, half = key
        first = "x" if color == 0 else "z"
        plan.append(("recv", sq - 1))
        size = {"x": NX, "z": NZ, "y": 2}[link[0]]
        whole = True
        if half is not None:
            spot = (color, oz % NZ, ox % NX)
            parts[spot] = parts.get(spot, 0) + 1
            whole = parts[spot] == 2
            if whole and link[0] == first:
                second = "z" if color == 0 else "x"
                for sign in "+-":
                    step = 1 if sign == "+" else -1
                    n_oz = oz - step if second == "z" else oz
                    n_ox = ox - step if second == "x" else ox
                    sid = push(second + sign, now, (color, n_oz, n_ox, None), 2)
                    plan.append(("send", sid, color, second + sign, oz, ox, None))
        else:
            emit(now, color, link, oz, ox)
        if whole:
            spot = (color, oz % NZ)
            count[spot] = count.get(spot, 0) + 1
            if count[spot] == NX:
                plan.append(("product", color, oz % NZ))
    return plan, seq[0], max(links.free.values())


CHUNKS = (4, 3, 5, 2, 6, 1, 7, 0)
CHUNK_US = 1.3


def ring(color, stage):
    axis = ("z", "x") if color == 0 else ("x", "z")
    return axis[stage - 1], {"x": NX, "z": NZ}[axis[stage - 1]]


def reduce_plan():
    width = {0: SPLIT, 1: 1024 - SPLIT}
    links = Links()
    needs = {}
    inst_of = {(0, 1): (2, 1, 3, 0), (1, 1): CHUNKS, (0, 2): (0,), (1, 2): (0,)}
    for color in (1, 0):
        for stage in (1, 2):
            axis, n = ring(color, stage)
            for inst in inst_of[color, stage]:
                for flow in (-1, 1):
                    for k in range(n // 2, 0, -1):
                        task = ("s", color, stage, flow, inst, k)
                        there = (flow * k) % n
                        if stage == 1:
                            dep = [("chunk", there if color == 0 else inst)]
                        else:
                            dep = [("q", color, 1, there)]
                        if k < n // 2:
                            dep.append(("got", color, stage, flow, inst, k + 1))
                        needs[task] = dep
                dep = [("got", color, stage, flow, inst, 1) for flow in (-1, 1)]
                if stage == 1:
                    dep.append(("chunk", 0 if color == 0 else inst))
                else:
                    dep.append(("q", color, 1, 0))
                needs[("q", color, stage, inst)] = dep
        needs[("y", color)] = [("q", color, 2, 0)]
        needs[("out", color)] = [("goty", color)]
    done = set()
    plan = []
    heap = []
    seq = [0]

    def post(t, event):
        seq[0] += 1
        heapq.heappush(heap, (t, seq[0], event))

    for i, oz in enumerate(CHUNKS):
        post(CHUNK_US * (i + 1), ("chunk", oz))
    sids = {}
    last = 0.0
    while heap:
        t, _, event = heapq.heappop(heap)
        last = t
        done.add(event)
        if event[0] == "chunk":
            plan.append(event)
        moved = True
        while moved:
            moved = False
            for task in list(needs):
                if all(d in done for d in needs[task]):
                    del needs[task]
                    plan.append(task)
                    moved = True
                    if task[0] == "s":
                        _, color, stage, flow, inst, k = task
                        axis, n = ring(color, stage)
                        halves = 1 if k == n // 2 else 2
                        arrive = links.send((axis, flow), t, halves * 64 * width[color] * 2)
                        post(arrive, ("got",) + task[1:])
                        sids[task] = len(sids)
                    elif task[0] == "y":
                        post(links.send("y", t, 64 * width[task[1]] * 2), ("goty", task[1]))
                        sids[task] = len(sids)
                    elif task[0] == "q":
                        done.add(task)
    return plan, sids, last


def send(src, dst, ssem, rsem, dev):
    c = pltpu.make_async_remote_copy(
        src_ref=src, dst_ref=dst, send_sem=ssem, recv_sem=rsem, device_id=dev, device_id_type=MESH
    )
    c.start()
    return c


def tdot(a, b):
    return lax.dot_general(a, b, (((0,), (0,)), ((), ())), preferred_element_type=F32)


def layer_kernel(
    gplan, rplan, sids, scale,
    code_ref, bound_ref, rv_ref, gb_ref, cs_ref, tok_hbm, q_hbm, k_hbm, gate_hbm, tgt_hbm,
    gated_hbm, out_ref,
    tok, q, k, gate, tgt, w_own, factor, wa, wb, acc, v, wts, qd, kd, go, ga, gv, hold, rates,
    packed, xbuf, pref, tbuf, ybuf, zbuf, rbuf, obuf, ebuf, sums, got, inv, inn,
    ra1, rb1, ra2, rb2, qa, qb, fa, fb, ya, yb, va, vb,
    lsem, gs, gr, s1, r1, s2, r2, s3, r3, s4, r4, ps, pr, rs, rr,
):
    x, y, z, wt = place()
    j = y * NZ + z
    rows = [lax.rem(x + n, NX) for n in range(1, NX)]
    cols = [lax.rem(j + n, NY * NZ) for n in range(1, NY * NZ)]
    row_dev = [at(p, y, z, wt) for p in rows]
    col_dev = [at(x, lax.div(p, NZ), lax.rem(p, NZ), wt) for p in cols]
    side_dev = [at(x, y, z, lax.rem(wt + n, 4)) for n in range(1, 4)]
    peers = {
        "x+": at(lax.rem(x + 1, NX), y, z, wt),
        "x-": at(lax.rem(x + NX - 1, NX), y, z, wt),
        "z+": at(x, y, lax.rem(z + 1, NZ), wt),
        "z-": at(x, y, lax.rem(z + NZ - 1, NZ), wt),
        "y": at(x, 1 - y, z, wt),
    }
    barrier = pltpu.get_barrier_semaphore()
    partners = row_dev + col_dev + side_dev
    for peer in partners:
        pl.semaphore_signal(barrier, inc=1, device_id=peer, device_id_type=MESH)
    loads = [
        pltpu.make_async_copy(a, b, lsem.at[n])
        for n, (a, b) in enumerate(
            [(tok_hbm, tok), (q_hbm, q), (k_hbm, k), (gate_hbm, gate), (tgt_hbm, tgt)]
        )
    ]
    for c in (1, 2, 0, 3, 4):
        loads[c].start()

    squash = jax.nn.sigmoid(rv_ref[...])
    raw = 1.2 * squash - 0.1
    w_own[...] = (
        cs_ref[...] * (gb_ref[...].astype(F32) + jnp.clip(raw, 0.0, 1.0))
    ).astype(BF)
    factor[...] = cs_ref[...] * jnp.where(
        (raw > 0.0) & (raw < 1.0), 1.2 * squash * (1.0 - squash), 0.0
    )
    pl.semaphore_wait(barrier, len(partners))

    def rate_of(h, shape):
        return jnp.exp2(jnp.full(shape, -code_ref[h].astype(F32), F32))

    mult = [1.0 - 0.5 * bound_ref[c].astype(F32) for c in range(2)]

    def head_tables(h):
        lo = h * HEAD
        rate = rate_of(h, (1, HEAD))
        row = lax.broadcasted_iota(jnp.int32, (GROUP, HEAD), 0).astype(F32)
        qdec = jnp.exp(-(row * rate))
        kdec = jnp.exp(-((GROUP - row) * rate))
        i = lax.broadcasted_iota(jnp.int32, (GROUP, GROUP), 0)
        o = lax.broadcasted_iota(jnp.int32, (GROUP, GROUP), 1)
        gap = (i - o).astype(F32)
        causal = jnp.where(
            gap >= 0.0, jnp.exp(-(jnp.maximum(gap, 0.0) * rate_of(h, (1, GROUP)))), 0.0
        )
        rates[h * 8 : h * 8 + 8] = jnp.broadcast_to(jnp.exp(-GROUP * rate)[None], (8, 1, HEAD))
        for c in range(2):
            r = slice(c * GROUP, c * GROUP + GROUP)
            qh = q[r, lo : lo + HEAD]
            kh = k[r, lo : lo + HEAD]
            score = lax.dot_general(qh, kh, (((1,), (1,)), ((), ())), preferred_element_type=F32)
            wts[c, h] = (score * causal).astype(BF)
            qd[r, lo : lo + HEAD] = (qh.astype(F32) * qdec).astype(BF)
            kd[r, lo : lo + HEAD] = (kh.astype(F32) * kdec).astype(BF)

    def open_gates():
        go[...] = jax.nn.sigmoid(gate[...].astype(F32))

    fillers = [functools.partial(head_tables, h) for h in range(8)] + [open_gates]
    ready = [False]

    def filler():
        if not fillers:
            return
        if not ready[0]:
            for c in (1, 2, 3):
                loads[c].wait()
            ready[0] = True
        fillers.pop(0)()

    buf = (wa, wb)
    copies = {}
    tok_ready = False
    for n, op in enumerate(gplan):
        if op[0] == "send":
            _, sid, color, link, oz, ox, half = op
            w = buf[color]
            if link == "y":
                lo, hi = LANES[color]
                src = w_own.at[:, lo:hi]
                dst = w.at[y, z, x]
            else:
                zz = lax.rem(z + (oz + 2 * NZ), NZ)
                xx = lax.rem(x + (ox + 2 * NX), NX)
                dst = w.at[:, zz, xx] if half is None else w.at[half, zz, xx]
                src = dst
            copies[sid] = send(src, dst, gs.at[sid], gr.at[sid], peers[link])
            if len(copies) == 2:
                wa[y, z, x] = w_own[:, :SPLIT]
                wb[y, z, x] = w_own[:, SPLIT:]
                acc[...] = jnp.zeros_like(acc)
        elif op[0] == "recv":
            copies[op[1]].wait_recv()
        else:
            if not tok_ready:
                loads[0].wait()
                tok_ready = True
            _, color, oz = op
            zz = lax.rem(z + oz, NZ)
            lo, hi = LANES[color]
            w = buf[color]

            @pl.loop(0, 4)
            def _(i, zz=zz, lo=lo, hi=hi, w=w):
                r = pl.ds(pl.multiple_of(i * 128, 128), 128)
                t0 = tok[r, pl.ds(pl.multiple_of(zz * 256, 256), 256)]
                t1 = tok[r, pl.ds(pl.multiple_of(zz * 256 + 2048, 256), 256)]
                acc[r, lo:hi] += jnp.dot(
                    t0, w[0, zz].reshape(256, hi - lo), preferred_element_type=F32
                ) + jnp.dot(t1, w[1, zz].reshape(256, hi - lo), preferred_element_type=F32)
        if n >= 12 and n % 8 == 4:
            filler()
    while fillers:
        filler()

    def scan(f, reverse, meanwhile):
        one = [
            send(packed.at[f, p], xbuf.at[f, x], s1.at[f, n], r1.at[f, n], d)
            for n, (p, d) in enumerate(zip(rows, row_dev))
        ]
        xbuf[f, x] = packed[f, x]
        meanwhile()
        rate = rates[pl.ds(x * 16, 16)]
        rate = rate * rate
        rate1 = rates[x * 16 + j]
        rate1 = rate1 * rate1
        rate4 = (rate1 * rate1) * (rate1 * rate1)
        for c in one:
            c.wait_recv()
        order = list(reversed(range(NX))) if reverse else list(range(NX))
        total = jnp.zeros((16, 16, 128), F32)
        m_all = jnp.ones((16, 128), F32)
        mults = []
        for i in order:
            pref[i] = total
            mults.append(m_all)
            m = xbuf[f, i, 16].astype(F32)
            total = (rate * m[None]) * total + xbuf[f, i, pl.ds(0, 16)].astype(F32)
            m_all = m_all * m
        tbuf[f, :, 0] = total.astype(BF)
        tbuf[f, :, 1] = jnp.broadcast_to(m_all.astype(BF)[None], (16, 16, 128))
        two = [
            send(tbuf.at[f, p], ybuf.at[f, j], s2.at[f, n], r2.at[f, n], d)
            for n, (p, d) in enumerate(zip(cols, col_dev))
        ]
        ybuf[f, j] = tbuf[f, j]
        for c in two:
            c.wait_recv()
        state = jnp.zeros((16, 128), F32)
        span = NY * NZ
        for i in reversed(range(span)) if reverse else range(span):
            zbuf[f, i] = state.astype(BF)
            state = (rate4 * ybuf[f, i, 1].astype(F32)) * state + ybuf[f, i, 0].astype(F32)
        three = [
            send(zbuf.at[f, p], rbuf.at[f, j], s3.at[f, n], r3.at[f, n], d)
            for n, (p, d) in enumerate(zip(cols, col_dev))
        ]
        rbuf[f, j] = zbuf[f, j]
        for c in three:
            c.wait_recv()
        entering = rbuf[f].astype(F32)
        grow = jnp.ones((16, 1, 128), F32)
        for n, i in enumerate(order):
            obuf[f, i] = (pref[i] + (grow * mults[n][None]) * entering).astype(BF)
            grow = grow * rate
        four = [
            send(obuf.at[f, p], ebuf.at[f, x], s4.at[f, n], r4.at[f, n], d)
            for n, (p, d) in enumerate(zip(rows, row_dev))
        ]
        ebuf[f, x] = obuf[f, x]
        for c in four:
            c.wait_recv()
        return one + two + three + four

    def pack(f, h, part):
        packed[f, h // 2, (h % 2) * 8 : (h % 2) * 8 + 8] = part.astype(BF).reshape(8, 16, 128)

    def entered(f, h):
        return ebuf[f, h // 2, (h % 2) * 8 : (h % 2) * 8 + 8].reshape(HEAD, HEAD).astype(F32)

    def span_of(c, h):
        return slice(c * GROUP, c * GROUP + GROUP), slice(h * HEAD, h * HEAD + HEAD)

    for f in range(2):
        for n in range(NX):
            packed[f, n, 16] = jnp.full((16, 128), mult[0] * mult[1], F32).astype(BF)
    for h in range(8):
        fade = rates[h * 8]
        for c in range(2):
            r, l = span_of(c, h)
            v[r, l] = acc[r, l].astype(BF)
        u0 = tdot(kd[span_of(0, h)], v[span_of(0, h)])
        u1 = tdot(kd[span_of(1, h)], v[span_of(1, h)])
        hold[h] = u0
        pack(0, h, (fade * mult[1]) * u0 + u1)

    def intra():
        for h in range(8):
            for c in range(2):
                r, l = span_of(c, h)
                acc[r, l] = jnp.dot(wts[c, h], v[r, l], preferred_element_type=F32)

    scans = scan(0, False, intra)

    sums[12:16] = jnp.zeros((4, 128), F32)
    loads[4].wait()
    for c in range(2):
        square = jnp.zeros((GROUP, HEAD), F32)
        opened = jnp.zeros((GROUP, HEAD), F32)
        cross = jnp.zeros((GROUP, HEAD), F32)
        for h in range(8):
            r, l = span_of(c, h)
            fade = rates[h * 8]
            if c == 0:
                state = mult[0] * entered(0, h)
            else:
                state = mult[1] * hold[h] + (fade * (mult[0] * mult[1])) * entered(0, h)
            attn = acc[r, l] + jnp.dot(qd[r, l], state.astype(BF), preferred_element_type=F32)
            acc[r, l] = attn
            gated = attn * go[r, l]
            square = square + attn * attn
            opened = opened + gated * gated
            cross = cross + gated * tgt[r, l].astype(F32)
        for kind, part in enumerate((square, opened, cross)):
            for b in range(2):
                block = part[b * 128 : b * 128 + 128].T
                n = kind * 4 + c * 2 + b
                sums[n : n + 1] = jnp.sum(block, axis=0, keepdims=True)
    side = [
        send(sums, got.at[wt], ps.at[n], pr.at[n], d) for n, d in enumerate(side_dev)
    ]
    got[wt] = sums[...]
    for c in side:
        c.wait_recv()
    total = (got[0] + got[1]) + (got[2] + got[3])
    width = HEADS * HEAD
    inv_row = 1.0 / jnp.sqrt(total[0:4] / width + epsilon)
    inner_row = (scale * (total[4:8] * inv_row - total[8:12]) * inv_row) / width
    for n in range(4):
        r = slice(n * 128, n * 128 + 128)
        inv[r] = jnp.broadcast_to(inv_row[n : n + 1], (128, 128)).T
        inn[r] = jnp.broadcast_to(inner_row[n : n + 1], (128, 128)).T
    out_buf = q
    for h in range(8):
        fade = rates[h * 8]
        for c in range(2):
            r, l = span_of(c, h)
            normed = acc[r, l] * inv[r]
            gate_open = go[r, l]
            gated = normed * gate_open
            out_buf[r, l] = gated.astype(BF)
            grad_normed = ((gated - tgt[r, l].astype(F32)) * scale) * gate_open
            ga[r, l] = ((grad_normed - normed * inn[r]) * inv[r]).astype(BF)
        c0 = tdot(qd[span_of(0, h)], ga[span_of(0, h)])
        c1 = tdot(qd[span_of(1, h)], ga[span_of(1, h)])
        hold[h] = c1
        pack(1, h, mult[0] * c0 + (fade * (mult[0] * mult[1])) * c1)
    store = pltpu.make_async_copy(out_buf, gated_hbm, lsem.at[5])
    store.start()

    def back_intra():
        for h in range(8):
            for c in range(2):
                r, l = span_of(c, h)
                acc[r, l] = tdot(wts[c, h], ga[r, l])
        for c in copies.values():
            c.wait_send()

    scans += scan(1, True, back_intra)
    for h in range(8):
        fade = rates[h * 8]
        for c in range(2):
            r, l = span_of(c, h)
            state = entered(1, h)
            if c == 0:
                state = mult[1] * hold[h] + (fade * mult[1]) * state
            gv[r, l] = (
                acc[r, l] + jnp.dot(kd[r, l], state.astype(BF), preferred_element_type=F32)
            ).astype(BF)

    mine = (wa, wb)
    queue = (qa, qb)
    slots = {(0, 1): ra1, (1, 1): rb1, (0, 2): ra2, (1, 2): rb2}
    full = (fa, fb)
    ysend = (ya, yb)
    yrecv = (va, vb)
    moves = {}

    def slot(color, stage, flow, inst, n):
        r = slots[color, stage]
        f = 0 if flow < 0 else 1
        return r.at[f, inst, n] if stage == 1 else r.at[f, n]

    def own(color, stage, inst, there):
        if stage == 2:
            return queue[color].at[there]
        oz, ox = (there, inst) if color == 0 else (inst, there)
        return mine[color].at[:, lax.rem(z + oz, NZ), lax.rem(x + ox, NX)]

    for op in rplan:
        if op[0] == "chunk":
            zz = lax.rem(z + op[1], NZ)

            @pl.loop(0, 4)
            def _(i, zz=zz):
                yy = lax.div(i, 2)
                b = lax.rem(i, 2)
                piece = tok[:, pl.ds(pl.multiple_of(yy * 2048 + zz * 256 + b * 128, 128), 128)]
                r = tdot(piece, gv[...]).astype(BF)
                for u in range(2):
                    wa[yy, zz, b * 2 + u] = r[u * 64 : u * 64 + 64, :SPLIT]
                    wb[yy, zz, b * 2 + u] = r[u * 64 : u * 64 + 64, SPLIT:]
        elif op[0] == "s":
            _, color, stage, flow, inst, n = op
            axis, size = ring(color, stage)
            half = 0 if flow < 0 else 1
            p = own(color, stage, inst, (flow * n) % size)
            if n == size // 2:
                src = p.at[half]
                dst = slot(color, stage, flow, inst, n - 1).at[half]
            else:
                moves["s", color, stage, flow, inst, n + 1].wait_recv()
                src = slot(color, stage, flow, inst, n)
                dst = slot(color, stage, flow, inst, n - 1)
                if n == size // 2 - 1:
                    src[half] = (src[half].astype(F32) + p[half].astype(F32)).astype(BF)
                    src[1 - half] = p[1 - half]
                else:
                    src[...] = (src[...].astype(F32) + p[...].astype(F32)).astype(BF)
            sid = sids[op]
            link = axis + ("+" if flow > 0 else "-")
            moves[op] = send(src, dst, rs.at[sid], rr.at[sid], peers[link])
        elif op[0] == "q":
            _, color, stage, inst = op
            for flow in (-1, 1):
                moves["s", color, stage, flow, inst, 1].wait_recv()
            low = slot(color, stage, -1, inst, 0)
            high = slot(color, stage, 1, inst, 0)
            p = own(color, stage, inst, 0)
            total = low[...].astype(F32) + high[...].astype(F32) + p[...].astype(F32)
            if stage == 1:
                queue[color][inst] = total.astype(BF)
            else:
                full[color][...] = total
        elif op[0] == "y":
            color = op[1]
            ysend[color][...] = full[color][1 - y].astype(BF)
            sid = sids[op]
            moves[op] = send(ysend[color], yrecv[color], rs.at[sid], rr.at[sid], peers["y"])
        else:
            color = op[1]
            moves["y", color].wait_recv()
            lo, hi = LANES[color]
            out_ref[:, lo:hi] = factor[:, lo:hi] * (
                full[color][y] + yrecv[color][...].astype(F32)
            )
    store.wait()
    for c in scans + side + list(moves.values()):
        c.wait_send()


def on_device(
    tokens, round_var, grid_base, col_scale, queries, keys, gates, target, decay_code, boundary
):
    gplan, gn, _ = gather_plan()
    rplan, sids, _ = reduce_plan()
    rn = len(sids)
    scale = loss_weight / math.sqrt(tokens.shape[0] * lax.axis_size("ctx"))
    a, b = SPLIT, 1024 - SPLIT
    vm = pl.BlockSpec(memory_space=pltpu.VMEM)
    sm = pl.BlockSpec(memory_space=pltpu.SMEM)
    hbm = pl.BlockSpec(memory_space=pl.ANY)
    V = pltpu.VMEM
    D = pltpu.SemaphoreType.DMA
    scratch = [
        V((512, 4096), BF),
        V((512, 1024), BF), V((512, 1024), BF), V((512, 1024), BF), V((512, 1024), BF),
        V((64, 1024), BF), V((64, 1024), F32),
        V((NY, NZ, NX, 64, a), BF), V((NY, NZ, NX, 64, b), BF),
        V((512, 1024), F32), V((512, 1024), BF),
        V((2, 8, GROUP, GROUP), BF), V((512, 1024), BF), V((512, 1024), BF),
        V((512, 1024), F32), V((512, 1024), BF), V((512, 1024), BF),
        V((8, HEAD, HEAD), F32), V((64, 1, 128), F32),
        V((2, NX, 17, 16, 128), BF), V((2, NX, 17, 16, 128), BF),
        V((NX, 16, 16, 128), F32),
        V((2, 16, 2, 16, 128), BF), V((2, 16, 2, 16, 128), BF),
        V((2, 16, 16, 128), BF), V((2, 16, 16, 128), BF),
        V((2, NX, 16, 16, 128), BF), V((2, NX, 16, 16, 128), BF),
        V((16, 128), F32), V((4, 16, 128), F32),
        V((512, 128), F32), V((512, 128), F32),
        V((2, NX, NZ // 2, NY, 64, a), BF), V((2, NZ, NX // 2, NY, 64, b), BF),
        V((2, NX // 2, NY, 64, a), BF), V((2, NZ // 2, NY, 64, b), BF),
        V((NX, NY, 64, a), BF), V((NZ, NY, 64, b), BF),
        V((NY, 64, a), F32), V((NY, 64, b), F32),
        V((64, a), BF), V((64, b), BF), V((64, a), BF), V((64, b), BF),
        D((6,)), D((gn,)), D((gn,)),
        D((2, 3)), D((2, 3)), D((2, 15)), D((2, 15)), D((2, 15)), D((2, 15)), D((2, 3)), D((2, 3)),
        D((3,)), D((3,)), D((rn,)), D((rn,)),
    ]
    return pl.pallas_call(
        functools.partial(layer_kernel, gplan, rplan, sids, scale),
        out_shape=(
            jax.ShapeDtypeStruct((512, 1024), BF),
            jax.ShapeDtypeStruct((64, 1024), F32),
        ),
        in_specs=[sm, sm, vm, vm, vm, hbm, hbm, hbm, hbm, hbm],
        out_specs=(hbm, vm),
        scratch_shapes=scratch,
        compiler_params=pltpu.CompilerParams(
            collective_id=0, has_side_effects=True, vmem_limit_bytes=62 * 2**20
        ),
        name="layer_step",
    )(
        decay_code, boundary, round_var, grid_base, col_scale.reshape(1, -1), tokens, queries,
        keys, gates, target,
    )


def solution(mesh):
    placed = (
        P("ctx", None),
        P("ctx", "wt"),
        P("ctx", "wt"),
        P("wt"),
        P("ctx", "wt"),
        P("ctx", "wt"),
        P("ctx", "wt"),
        P("ctx", "wt"),
        P("wt"),
        P("ctx"),
    )
    return jax.shard_map(
        on_device,
        mesh=mesh,
        in_specs=placed,
        out_specs=(P("ctx", "wt"), P("ctx", "wt")),
        check_vma=False,
    )
```

```python
import functools, heapq, math
import jax
import jax.numpy as jnp
from jax import lax
from jax.sharding import PartitionSpec as P
from jax.experimental import pallas as pl
from jax.experimental.pallas import tpu as pltpu

MESH = pl.DeviceIdType.MESH
NX, NZ, NY = 4, 8, 2
SPLIT = 384
HEADS = 32
HEAD = 128
GROUP = 256
LANES = ((0, SPLIT), (SPLIT, 1024))
epsilon = 1e-06
loss_weight = 1024.0
BF = jnp.bfloat16
F32 = jnp.float32


def place():
    ctx = lax.axis_index("ctx")
    wt = lax.axis_index("wt")
    x = lax.rem(ctx, NX)
    z = lax.rem(lax.div(ctx, NX), NZ)
    y = lax.div(ctx, NX * NZ)
    return x, y, z, wt


def at(x, y, z, wt):
    return (y * (NX * NZ) + z * NX + x, wt)


LAT = 1.7
RATE = 90e3 / 2


class Links:
    def __init__(self):
        self.free = {}

    def send(self, link, now, nbytes):
        start = max(now, self.free.get(link, 0.0))
        done = start + nbytes / RATE
        self.free[link] = done
        return done + LAT


def gather_plan():
    width = {0: SPLIT, 1: 1024 - SPLIT}
    links = Links()
    heap = []
    plan = []
    seq = [0]
    have = {}

    def push(link, now, key, halves):
        color, oz, ox, _ = key
        nbytes = halves * 64 * width[color] * 2
        seq[0] += 1
        heapq.heappush(heap, (links.send(link, now, nbytes), seq[0], link, key))
        return seq[0] - 1

    def sends_for(color, link, oz, ox):
        out = []
        axis = link[0]
        first, second = ("x", "z") if color == 0 else ("z", "x")
        size = {"x": NX, "z": NZ}
        off = {"x": ox, "z": oz}
        if axis in "xz":
            dist = abs(off[axis])
            if dist < size[axis] // 2:
                out.append((link, 0 if link[1] == "+" else 1) if dist == size[axis] // 2 - 1 else (link, None))
        if axis == "y":
            out += [(first + "+", None), (first + "-", None)]
        if axis in ("y", first):
            out += [(second + "+", None), (second + "-", None)]
        return out

    def emit(now, color, link, oz, ox, skip_second=False):
        for nxt, half in sends_for(color, link, oz, ox):
            if skip_second and nxt[0] != link[0]:
                continue
            step = 1 if nxt[1] == "+" else -1
            n_oz = oz - step if nxt[0] == "z" else oz
            n_ox = ox - step if nxt[0] == "x" else ox
            sid = push(nxt, now, (color, n_oz, n_ox, half), 1 if half is not None else 2)
            plan.append(("send", sid, color, nxt, oz, ox, half))

    for color in (1, 0):
        sid = push("y", 0.0, (color, 0, 0, None), 1)
        plan.append(("send", sid, color, "y", 0, 0, None))
    count = {}
    parts = {}
    while heap:
        now, sq, link, key = heapq.heappop(heap)
        color, oz, ox, half = key
        first = "x" if color == 0 else "z"
        plan.append(("recv", sq - 1))
        size = {"x": NX, "z": NZ, "y": 2}[link[0]]
        whole = True
        if half is not None:
            spot = (color, oz % NZ, ox % NX)
            parts[spot] = parts.get(spot, 0) + 1
            whole = parts[spot] == 2
            if whole and link[0] == first:
                second = "z" if color == 0 else "x"
                for sign in "+-":
                    step = 1 if sign == "+" else -1
                    n_oz = oz - step if second == "z" else oz
                    n_ox = ox - step if second == "x" else ox
                    sid = push(second + sign, now, (color, n_oz, n_ox, None), 2)
                    plan.append(("send", sid, color, second + sign, oz, ox, None))
        else:
            emit(now, color, link, oz, ox)
        if whole:
            spot = (color, oz % NZ)
            count[spot] = count.get(spot, 0) + 1
            if count[spot] == NX:
                plan.append(("product", color, oz % NZ))
    return plan, seq[0], max(links.free.values())


COLOURS = (
    (0, 256, False, "x"),
    (256, 512, True, "z"),
    (512, 896, True, "x"),
    (896, 1024, True, "z"),
)
CHUNKS = (4, 3, 5, 2, 6, 1, 7, 0)
CHUNK_US = 1.3

def ring(first, stage):
    axis = first if stage == 1 else ("x" if first == "z" else "z")
    return axis, {"x": NX, "z": NZ}[axis]


def reduce_plan(colours):
    links = Links()
    needs = {}
    for color, (lo, hi, paired, first) in enumerate(colours):
        for stage in (1, 2):
            axis, n = ring(first, stage)
            insts = (0,) if stage == 2 else (2, 1, 3, 0) if first == "z" else CHUNKS
            for inst in insts:
                for flow in (-1, 1):
                    for k in range(n // 2, 0, -1):
                        there = (flow * k) % n
                        if stage == 1:
                            dep = [("chunk", color, there if first == "z" else inst)]
                        else:
                            dep = [("q", color, 1, there)]
                        if k < n // 2:
                            dep.append(("got", color, stage, flow, inst, k + 1))
                        needs["s", color, stage, flow, inst, k] = dep
                dep = [("got", color, stage, flow, inst, 1) for flow in (-1, 1)]
                dep.append(("chunk", color, 0 if first == "z" else inst) if stage == 1 else ("q", color, 1, 0))
                needs["q", color, stage, inst] = dep
        if not paired:
            needs["y", color] = [("q", color, 2, 0)]
            needs["out", color] = [("goty", color)]
    done = set()
    plan = []
    heap = []
    seq = [0]

    def post(t, event):
        seq[0] += 1
        heapq.heappush(heap, (t, seq[0], event))

    core = 0.0
    for color, (lo, hi, paired, _) in enumerate(colours):
        if paired:
            core = max(core, links.send("y", 0.0, 512 * (hi - lo) * 2))
        for oz in CHUNKS:
            core += CHUNK_US * (hi - lo) / 1024
            post(core, ("chunk", color, oz))
    sids = {}
    last = 0.0
    while heap:
        t, _, event = heapq.heappop(heap)
        last = t
        done.add(event)
        if event[0] == "chunk":
            plan.append(event)
        moved = True
        while moved:
            moved = False
            for task in list(needs):
                if not all(d in done for d in needs[task]):
                    continue
                del needs[task]
                plan.append(task)
                moved = True
                width = colours[task[1]][1] - colours[task[1]][0]
                rows = 32 if colours[task[1]][2] else 64
                if task[0] == "s":
                    _, color, stage, flow, inst, k = task
                    axis, n = ring(colours[color][3], stage)
                    halves = 1 if k == n // 2 else 2
                    post(links.send((axis, flow), t, halves * rows * width * 2), ("got",) + task[1:])
                    sids[task] = len(sids)
                elif task[0] == "y":
                    post(links.send("y", t, 64 * width * 2), ("goty", task[1]))
                    sids[task] = len(sids)
                elif task[0] == "q":
                    done.add(task)
    return plan, sids, last


def send(src, dst, ssem, rsem, dev):
    c = pltpu.make_async_remote_copy(
        src_ref=src, dst_ref=dst, send_sem=ssem, recv_sem=rsem, device_id=dev, device_id_type=MESH
    )
    c.start()
    return c


def tdot(a, b):
    return lax.dot_general(a, b, (((0,), (0,)), ((), ())), preferred_element_type=F32)


def layer_kernel(
    gplan, rplan, sids, scale,
    code_ref, bound_ref, rv_ref, gb_ref, cs_ref, tok_hbm, q_hbm, k_hbm, gate_hbm, tgt_hbm,
    gated_hbm, out_ref,
    tok, q, k, gate, tgt, w_own, factor, wa, wb, acc, v, wts, qd, kd, go, ga, gv, hold, rates,
    packed, xbuf, pref, tbuf, ybuf, zbuf, rbuf, obuf, ebuf, sums, got, inv, inn,
    tp, gp,
    lsem, gs, gr, s1, r1, s2, r2, s3, r3, s4, r4, ps, pr, rs, rr, ts, tr, us, ur, hs, hr,
    *lots,
):
    x, y, z, wt = place()
    j = y * NZ + z
    rows = [lax.rem(x + n, NX) for n in range(1, NX)]
    cols = [lax.rem(j + n, NY * NZ) for n in range(1, NY * NZ)]
    row_dev = [at(p, y, z, wt) for p in rows]
    col_dev = [at(x, lax.div(p, NZ), lax.rem(p, NZ), wt) for p in cols]
    side_dev = [at(x, y, z, lax.rem(wt + n, 4)) for n in range(1, 4)]
    peers = {
        "x+": at(lax.rem(x + 1, NX), y, z, wt),
        "x-": at(lax.rem(x + NX - 1, NX), y, z, wt),
        "z+": at(x, y, lax.rem(z + 1, NZ), wt),
        "z-": at(x, y, lax.rem(z + NZ - 1, NZ), wt),
        "y": at(x, 1 - y, z, wt),
    }
    barrier = pltpu.get_barrier_semaphore()
    partners = row_dev + col_dev + side_dev
    for peer in partners:
        pl.semaphore_signal(barrier, inc=1, device_id=peer, device_id_type=MESH)
    loads = [
        pltpu.make_async_copy(a, b, lsem.at[n])
        for n, (a, b) in enumerate(
            [(tok_hbm, tok), (q_hbm, q), (k_hbm, k), (gate_hbm, gate), (tgt_hbm, tgt)]
        )
    ]
    for c in (1, 2, 0, 3, 4):
        loads[c].start()

    squash = jax.nn.sigmoid(rv_ref[...])
    raw = 1.2 * squash - 0.1
    w_own[...] = (
        cs_ref[...] * (gb_ref[...].astype(F32) + jnp.clip(raw, 0.0, 1.0))
    ).astype(BF)
    factor[...] = cs_ref[...] * jnp.where(
        (raw > 0.0) & (raw < 1.0), 1.2 * squash * (1.0 - squash), 0.0
    )
    pl.semaphore_wait(barrier, len(partners))

    def rate_of(h, shape):
        return jnp.exp2(jnp.full(shape, -code_ref[h].astype(F32), F32))

    mult = [1.0 - 0.5 * bound_ref[c].astype(F32) for c in range(2)]

    def head_tables(h):
        lo = h * HEAD
        rate = rate_of(h, (1, HEAD))
        row = lax.broadcasted_iota(jnp.int32, (GROUP, HEAD), 0).astype(F32)
        qdec = jnp.exp(-(row * rate))
        kdec = jnp.exp(-((GROUP - row) * rate))
        i = lax.broadcasted_iota(jnp.int32, (GROUP, GROUP), 0)
        o = lax.broadcasted_iota(jnp.int32, (GROUP, GROUP), 1)
        gap = (i - o).astype(F32)
        causal = jnp.where(
            gap >= 0.0, jnp.exp(-(jnp.maximum(gap, 0.0) * rate_of(h, (1, GROUP)))), 0.0
        )
        rates[h * 8 : h * 8 + 8] = jnp.broadcast_to(jnp.exp(-GROUP * rate)[None], (8, 1, HEAD))
        for c in range(2):
            r = slice(c * GROUP, c * GROUP + GROUP)
            qh = q[r, lo : lo + HEAD]
            kh = k[r, lo : lo + HEAD]
            score = lax.dot_general(qh, kh, (((1,), (1,)), ((), ())), preferred_element_type=F32)
            wts[c, h] = (score * causal).astype(BF)
            qd[r, lo : lo + HEAD] = (qh.astype(F32) * qdec).astype(BF)
            kd[r, lo : lo + HEAD] = (kh.astype(F32) * kdec).astype(BF)

    def open_gates():
        go[...] = jax.nn.sigmoid(gate[...].astype(F32))

    fillers = [functools.partial(head_tables, h) for h in range(8)] + [open_gates]
    ready = [False]

    def filler():
        if not fillers:
            return
        if not ready[0]:
            for c in (1, 2, 3):
                loads[c].wait()
            ready[0] = True
        fillers.pop(0)()

    buf = (wa, wb)
    copies = {}
    tok_ready = False
    for n, op in enumerate(gplan):
        if op[0] == "send":
            _, sid, color, link, oz, ox, half = op
            w = buf[color]
            if link == "y":
                lo, hi = LANES[color]
                src = w_own.at[:, lo:hi]
                dst = w.at[y, z, x]
            else:
                zz = lax.rem(z + (oz + 2 * NZ), NZ)
                xx = lax.rem(x + (ox + 2 * NX), NX)
                dst = w.at[:, zz, xx] if half is None else w.at[half, zz, xx]
                src = dst
            copies[sid] = send(src, dst, gs.at[sid], gr.at[sid], peers[link])
            if len(copies) == 2:
                wa[y, z, x] = w_own[:, :SPLIT]
                wb[y, z, x] = w_own[:, SPLIT:]
                acc[...] = jnp.zeros_like(acc)
        elif op[0] == "recv":
            copies[op[1]].wait_recv()
        else:
            if not tok_ready:
                loads[0].wait()
                tok_ready = True
            _, color, oz = op
            zz = lax.rem(z + oz, NZ)
            lo, hi = LANES[color]
            w = buf[color]

            @pl.loop(0, 4)
            def _(i, zz=zz, lo=lo, hi=hi, w=w):
                r = pl.ds(pl.multiple_of(i * 128, 128), 128)
                t0 = tok[r, pl.ds(pl.multiple_of(zz * 256, 256), 256)]
                t1 = tok[r, pl.ds(pl.multiple_of(zz * 256 + 2048, 256), 256)]
                acc[r, lo:hi] += jnp.dot(
                    t0, w[0, zz].reshape(256, hi - lo), preferred_element_type=F32
                ) + jnp.dot(t1, w[1, zz].reshape(256, hi - lo), preferred_element_type=F32)
        if n >= 12 and n % 8 == 4:
            filler()
    while fillers:
        filler()

    core = lax.rem(wt, 2)
    twin = at(x, y, z, wt + 1 - 2 * core)
    trade = []

    def trade_tokens(first, last):
        for n in range(first, last):
            r = pl.ds(pl.multiple_of(core * 256 + n * 32, 32), 32)
            src = tok.at[r, pl.ds(pl.multiple_of((1 - y) * 2048, 2048), 2048)]
            trade.append(send(src, tp.at[r], ts.at[n], tr.at[n], peers["y"]))

    trade_tokens(0, 2)

    def scan(f, reverse, meanwhile, later):
        one = [
            send(packed.at[f, p], xbuf.at[f, x], s1.at[f, n], r1.at[f, n], d)
            for n, (p, d) in enumerate(zip(rows, row_dev))
        ]
        xbuf[f, x] = packed[f, x]
        meanwhile()
        rate = rates[pl.ds(x * 16, 16)]
        rate = rate * rate
        rate1 = rates[x * 16 + j]
        rate1 = rate1 * rate1
        rate4 = (rate1 * rate1) * (rate1 * rate1)
        for c in one:
            c.wait_recv()
        order = list(reversed(range(NX))) if reverse else list(range(NX))
        total = jnp.zeros((16, 16, 128), F32)
        m_all = jnp.ones((16, 128), F32)
        mults = []
        for i in order:
            pref[i] = total
            mults.append(m_all)
            m = xbuf[f, i, 16].astype(F32)
            total = (rate * m[None]) * total + xbuf[f, i, pl.ds(0, 16)].astype(F32)
            m_all = m_all * m
        tbuf[f, :, 0] = total.astype(BF)
        tbuf[f, :, 1] = jnp.broadcast_to(m_all.astype(BF)[None], (16, 16, 128))
        two = [
            send(tbuf.at[f, p], ybuf.at[f, j], s2.at[f, n], r2.at[f, n], d)
            for n, (p, d) in enumerate(zip(cols, col_dev))
        ]
        ybuf[f, j] = tbuf[f, j]
        for c in two:
            c.wait_recv()
        state = jnp.zeros((16, 128), F32)
        span = NY * NZ
        for i in reversed(range(span)) if reverse else range(span):
            zbuf[f, i] = state.astype(BF)
            state = (rate4 * ybuf[f, i, 1].astype(F32)) * state + ybuf[f, i, 0].astype(F32)
        three = [
            send(zbuf.at[f, p], rbuf.at[f, j], s3.at[f, n], r3.at[f, n], d)
            for n, (p, d) in enumerate(zip(cols, col_dev))
        ]
        rbuf[f, j] = zbuf[f, j]
        for c in three:
            c.wait_recv()
        later()
        entering = rbuf[f].astype(F32)
        grow = jnp.ones((16, 1, 128), F32)
        for n, i in enumerate(order):
            obuf[f, i] = (pref[i] + (grow * mults[n][None]) * entering).astype(BF)
            grow = grow * rate
        four = [
            send(obuf.at[f, p], ebuf.at[f, x], s4.at[f, n], r4.at[f, n], d)
            for n, (p, d) in enumerate(zip(rows, row_dev))
        ]
        ebuf[f, x] = obuf[f, x]
        for c in four:
            c.wait_recv()
        return one + two + three + four

    def pack(f, h, part):
        packed[f, h // 2, (h % 2) * 8 : (h % 2) * 8 + 8] = part.astype(BF).reshape(8, 16, 128)

    def entered(f, h):
        return ebuf[f, h // 2, (h % 2) * 8 : (h % 2) * 8 + 8].reshape(HEAD, HEAD).astype(F32)

    def span_of(c, h):
        return slice(c * GROUP, c * GROUP + GROUP), slice(h * HEAD, h * HEAD + HEAD)

    for f in range(2):
        for n in range(NX):
            packed[f, n, 16] = jnp.full((16, 128), mult[0] * mult[1], F32).astype(BF)
    for h in range(8):
        fade = rates[h * 8]
        for c in range(2):
            r, l = span_of(c, h)
            v[r, l] = acc[r, l].astype(BF)
        u0 = tdot(kd[span_of(0, h)], v[span_of(0, h)])
        u1 = tdot(kd[span_of(1, h)], v[span_of(1, h)])
        hold[h] = u0
        pack(0, h, (fade * mult[1]) * u0 + u1)

    def intra():
        for h in range(8):
            for c in range(2):
                r, l = span_of(c, h)
                acc[r, l] = jnp.dot(wts[c, h], v[r, l], preferred_element_type=F32)

    scans = scan(0, False, intra, lambda: trade_tokens(2, 8))

    sums[12:16] = jnp.zeros((4, 128), F32)
    loads[4].wait()
    for c in range(2):
        square = jnp.zeros((GROUP, HEAD), F32)
        opened = jnp.zeros((GROUP, HEAD), F32)
        cross = jnp.zeros((GROUP, HEAD), F32)
        for h in range(8):
            r, l = span_of(c, h)
            fade = rates[h * 8]
            if c == 0:
                state = mult[0] * entered(0, h)
            else:
                state = mult[1] * hold[h] + (fade * (mult[0] * mult[1])) * entered(0, h)
            attn = acc[r, l] + jnp.dot(qd[r, l], state.astype(BF), preferred_element_type=F32)
            acc[r, l] = attn
            gated = attn * go[r, l]
            square = square + attn * attn
            opened = opened + gated * gated
            cross = cross + gated * tgt[r, l].astype(F32)
        for kind, part in enumerate((square, opened, cross)):
            for b in range(2):
                block = part[b * 128 : b * 128 + 128].T
                n = kind * 4 + c * 2 + b
                sums[n : n + 1] = jnp.sum(block, axis=0, keepdims=True)
    side = [
        send(sums, got.at[wt], ps.at[n], pr.at[n], d) for n, d in enumerate(side_dev)
    ]
    got[wt] = sums[...]
    for c in side:
        c.wait_recv()
    total = (got[0] + got[1]) + (got[2] + got[3])
    width = HEADS * HEAD
    inv_row = 1.0 / jnp.sqrt(total[0:4] / width + epsilon)
    inner_row = (scale * (total[4:8] * inv_row - total[8:12]) * inv_row) / width
    for n in range(4):
        r = slice(n * 128, n * 128 + 128)
        inv[r] = jnp.broadcast_to(inv_row[n : n + 1], (128, 128)).T
        inn[r] = jnp.broadcast_to(inner_row[n : n + 1], (128, 128)).T
    out_buf = q
    for h in range(8):
        fade = rates[h * 8]
        for c in range(2):
            r, l = span_of(c, h)
            normed = acc[r, l] * inv[r]
            gate_open = go[r, l]
            gated = normed * gate_open
            out_buf[r, l] = gated.astype(BF)
            grad_normed = ((gated - tgt[r, l].astype(F32)) * scale) * gate_open
            ga[r, l] = ((grad_normed - normed * inn[r]) * inv[r]).astype(BF)
        c0 = tdot(qd[span_of(0, h)], ga[span_of(0, h)])
        c1 = tdot(qd[span_of(1, h)], ga[span_of(1, h)])
        hold[h] = c1
        pack(1, h, mult[0] * c0 + (fade * (mult[0] * mult[1])) * c1)
    store = pltpu.make_async_copy(out_buf, gated_hbm, lsem.at[5])
    store.start()

    def back_intra():
        for h in range(8):
            for c in range(2):
                r, l = span_of(c, h)
                acc[r, l] = tdot(wts[c, h], ga[r, l])
        for n, c in enumerate(trade):
            c.wait_recv()
            r = pl.ds(pl.multiple_of(core * 256 + n * 32, 32), 32)
            share.append(send(tp.at[r], tp.at[r], us.at[n], ur.at[n], twin))

    share = []
    scans += scan(1, True, back_intra, lambda: None)
    grads = {}

    def value_grads(h):
        fade = rates[h * 8]
        for c in range(2):
            r, l = span_of(c, h)
            state = entered(1, h)
            if c == 0:
                state = mult[1] * hold[h] + (fade * mult[1]) * state
            gv[r, l] = (
                acc[r, l] + jnp.dot(kd[r, l], state.astype(BF), preferred_element_type=F32)
            ).astype(BF)

    for color, (lo, hi, paired, _) in sorted(enumerate(COLOURS), key=lambda e: not e[1][2]):
        for h in range(lo // HEAD, hi // HEAD):
            value_grads(h)
        if paired:
            grads[color] = send(
                gv.at[:, lo:hi], gp.at[:, lo:hi], hs.at[color], hr.at[color], peers["y"]
            )

    bufs = [lots[n : n + 7] for n in range(0, len(lots), 7)]
    moves = {}
    arrived = set()

    def slot(color, stage, flow, inst, n):
        r = bufs[color][stage]
        f = 0 if flow < 0 else 1
        return r.at[f, inst, n] if stage == 1 else r.at[f, n]

    def own(color, stage, inst, there):
        if stage == 2:
            return bufs[color][3].at[there]
        oz, ox = (there, inst) if COLOURS[color][3] == "z" else (inst, there)
        return bufs[color][0].at[lax.rem(z + oz, NZ), lax.rem(x + ox, NX)]

    for op in rplan:
        color = op[1]
        lo, hi, paired, first = COLOURS[color]
        if op[0] == "chunk":
            zz = lax.rem(z + op[2], NZ)
            part = bufs[color][0]
            if paired:
                if not arrived:
                    for c in share:
                        c.wait_recv()
                if color not in arrived:
                    grads[color].wait_recv()
                    arrived.add(color)

                @pl.loop(0, 2)
                def _(b, zz=zz, lo=lo, hi=hi, part=part):
                    mine = tok[:, pl.ds(pl.multiple_of(y * 2048 + zz * 256 + b * 128, 128), 128)]
                    other = tp[:, pl.ds(pl.multiple_of(zz * 256 + b * 128, 128), 128)]
                    r = (tdot(mine, gv[:, lo:hi]) + tdot(other, gp[:, lo:hi])).astype(BF)
                    for u in range(2):
                        part[zz, b * 2 + u] = r[u * 64 : u * 64 + 64].reshape(2, 32, hi - lo)
            else:

                @pl.loop(0, 4)
                def _(i, zz=zz, lo=lo, hi=hi, part=part):
                    yy = lax.div(i, 2)
                    b = lax.rem(i, 2)
                    mine = tok[:, pl.ds(pl.multiple_of(yy * 2048 + zz * 256 + b * 128, 128), 128)]
                    r = tdot(mine, gv[:, lo:hi]).astype(BF)
                    for u in range(2):
                        part[zz, b * 2 + u, yy] = r[u * 64 : u * 64 + 64]
        elif op[0] == "s":
            _, color, stage, flow, inst, n = op
            axis, size = ring(first, stage)
            half = 0 if flow < 0 else 1
            p = own(color, stage, inst, (flow * n) % size)
            if n == size // 2:
                src = p.at[half]
                dst = slot(color, stage, flow, inst, n - 1).at[half]
            else:
                moves["s", color, stage, flow, inst, n + 1].wait_recv()
                src = slot(color, stage, flow, inst, n)
                dst = slot(color, stage, flow, inst, n - 1)
                if n == size // 2 - 1:
                    src[half] = (src[half].astype(F32) + p[half].astype(F32)).astype(BF)
                    src[1 - half] = p[1 - half]
                else:
                    src[...] = (src[...].astype(F32) + p[...].astype(F32)).astype(BF)
            sid = sids[op]
            link = axis + ("+" if flow > 0 else "-")
            moves[op] = send(src, dst, rs.at[sid], rr.at[sid], peers[link])
        elif op[0] == "q":
            _, color, stage, inst = op
            for flow in (-1, 1):
                moves["s", color, stage, flow, inst, 1].wait_recv()
            low = slot(color, stage, -1, inst, 0)
            high = slot(color, stage, 1, inst, 0)
            p = own(color, stage, inst, 0)
            total = low[...].astype(F32) + high[...].astype(F32) + p[...].astype(F32)
            if stage == 1:
                bufs[color][3][inst] = total.astype(BF)
            elif paired:
                out_ref[:, lo:hi] = factor[:, lo:hi] * total.reshape(64, hi - lo)
            else:
                bufs[color][4][...] = total
        elif op[0] == "y":
            ysend, yrecv = bufs[color][5:7]
            ysend[...] = bufs[color][4][1 - y].astype(BF)
            sid = sids[op]
            moves[op] = send(ysend, yrecv, rs.at[sid], rr.at[sid], peers["y"])
        else:
            moves["y", color].wait_recv()
            out_ref[:, lo:hi] = factor[:, lo:hi] * (
                bufs[color][4][y] + bufs[color][6][...].astype(F32)
            )
    store.wait()
    for c in list(copies.values()) + scans + side + trade + share:
        c.wait_send()
    for c in list(grads.values()) + list(moves.values()):
        c.wait_send()


def on_device(
    tokens, round_var, grid_base, col_scale, queries, keys, gates, target, decay_code, boundary
):
    gplan, gn, _ = gather_plan()
    rplan, sids, _ = reduce_plan(COLOURS)
    rn = len(sids)
    scale = loss_weight / math.sqrt(tokens.shape[0] * lax.axis_size("ctx"))
    a, b = SPLIT, 1024 - SPLIT
    vm = pl.BlockSpec(memory_space=pltpu.VMEM)
    sm = pl.BlockSpec(memory_space=pltpu.SMEM)
    hbm = pl.BlockSpec(memory_space=pl.ANY)
    V = pltpu.VMEM
    D = pltpu.SemaphoreType.DMA
    scratch = [
        V((512, 4096), BF),
        V((512, 1024), BF), V((512, 1024), BF), V((512, 1024), BF), V((512, 1024), BF),
        V((64, 1024), BF), V((64, 1024), F32),
        V((NY, NZ, NX, 64, a), BF), V((NY, NZ, NX, 64, b), BF),
        V((512, 1024), F32), V((512, 1024), BF),
        V((2, 8, GROUP, GROUP), BF), V((512, 1024), BF), V((512, 1024), BF),
        V((512, 1024), F32), V((512, 1024), BF), V((512, 1024), BF),
        V((8, HEAD, HEAD), F32), V((64, 1, 128), F32),
        V((2, NX, 17, 16, 128), BF), V((2, NX, 17, 16, 128), BF),
        V((NX, 16, 16, 128), F32),
        V((2, 16, 2, 16, 128), BF), V((2, 16, 2, 16, 128), BF),
        V((2, 16, 16, 128), BF), V((2, 16, 16, 128), BF),
        V((2, NX, 16, 16, 128), BF), V((2, NX, 16, 16, 128), BF),
        V((16, 128), F32), V((4, 16, 128), F32),
        V((512, 128), F32), V((512, 128), F32),
        V((512, 2048), BF), V((512, 1024), BF),
        D((6,)), D((gn,)), D((gn,)),
        D((2, 3)), D((2, 3)), D((2, 15)), D((2, 15)), D((2, 15)), D((2, 15)), D((2, 3)), D((2, 3)),
        D((3,)), D((3,)), D((rn,)), D((rn,)),
        D((8,)), D((8,)), D((8,)), D((8,)), D((len(COLOURS),)), D((len(COLOURS),)),
    ]
    for lo, hi, paired, first in COLOURS:
        r, w = 32 if paired else 64, hi - lo
        n1, n2 = (NX, NZ) if first == "z" else (NZ, NX)
        f = 8 if paired else 64
        scratch += [
            V((NZ, NX, 2, r, w), BF), V((2, n1, n2 // 2, 2, r, w), BF),
            V((2, n1 // 2, 2, r, w), BF), V((n1, 2, r, w), BF),
            V((2, f, w), F32), V((f, w), BF), V((f, w), BF),
        ]
    return pl.pallas_call(
        functools.partial(layer_kernel, gplan, rplan, sids, scale),
        out_shape=(
            jax.ShapeDtypeStruct((512, 1024), BF),
            jax.ShapeDtypeStruct((64, 1024), F32),
        ),
        in_specs=[sm, sm, vm, vm, vm, hbm, hbm, hbm, hbm, hbm],
        out_specs=(hbm, vm),
        scratch_shapes=scratch,
        compiler_params=pltpu.CompilerParams(
            collective_id=0, has_side_effects=True, vmem_limit_bytes=62 * 2**20
        ),
        name="layer_step",
    )(
        decay_code, boundary, round_var, grid_base, col_scale.reshape(1, -1), tokens, queries,
        keys, gates, target,
    )


def solution(mesh):
    placed = (
        P("ctx", None),
        P("ctx", "wt"),
        P("ctx", "wt"),
        P("wt"),
        P("ctx", "wt"),
        P("ctx", "wt"),
        P("ctx", "wt"),
        P("ctx", "wt"),
        P("wt"),
        P("ctx"),
    )
    return jax.shard_map(
        on_device,
        mesh=mesh,
        in_specs=placed,
        out_specs=(P("ctx", "wt"), P("ctx", "wt")),
        check_vma=False,
    )
```

```python
import functools, heapq, math
import jax
import jax.numpy as jnp
from jax import lax
from jax.sharding import PartitionSpec as P
from jax.experimental import pallas as pl
from jax.experimental.pallas import tpu as pltpu

MESH = pl.DeviceIdType.MESH
NX, NZ, NY = 4, 8, 2
SPLIT = 384
HEADS = 32
HEAD = 128
GROUP = 256
LANES = ((0, SPLIT), (SPLIT, 1024))
epsilon = 1e-06
loss_weight = 1024.0
BF = jnp.bfloat16
F32 = jnp.float32


def place():
    ctx = lax.axis_index("ctx")
    wt = lax.axis_index("wt")
    x = lax.rem(ctx, NX)
    z = lax.rem(lax.div(ctx, NX), NZ)
    y = lax.div(ctx, NX * NZ)
    return x, y, z, wt


def at(x, y, z, wt):
    return (y * (NX * NZ) + z * NX + x, wt)


LAT = 1.7
RATE = 90e3 / 2


class Links:
    def __init__(self):
        self.free = {}

    def send(self, link, now, nbytes):
        start = max(now, self.free.get(link, 0.0))
        done = start + nbytes / RATE
        self.free[link] = done
        return done + LAT


def gather_plan():
    width = {0: SPLIT, 1: 1024 - SPLIT}
    links = Links()
    heap = []
    plan = []
    seq = [0]
    have = {}

    def push(link, now, key, halves):
        color, oz, ox, _ = key
        nbytes = halves * 64 * width[color] * 2
        seq[0] += 1
        heapq.heappush(heap, (links.send(link, now, nbytes), seq[0], link, key))
        return seq[0] - 1

    def sends_for(color, link, oz, ox):
        out = []
        axis = link[0]
        first, second = ("x", "z") if color == 0 else ("z", "x")
        size = {"x": NX, "z": NZ}
        off = {"x": ox, "z": oz}
        if axis in "xz":
            dist = abs(off[axis])
            if dist < size[axis] // 2:
                out.append((link, 0 if link[1] == "+" else 1) if dist == size[axis] // 2 - 1 else (link, None))
        if axis == "y":
            out += [(first + "+", None), (first + "-", None)]
        if axis in ("y", first):
            out += [(second + "+", None), (second + "-", None)]
        return out

    def emit(now, color, link, oz, ox, skip_second=False):
        for nxt, half in sends_for(color, link, oz, ox):
            if skip_second and nxt[0] != link[0]:
                continue
            step = 1 if nxt[1] == "+" else -1
            n_oz = oz - step if nxt[0] == "z" else oz
            n_ox = ox - step if nxt[0] == "x" else ox
            sid = push(nxt, now, (color, n_oz, n_ox, half), 1 if half is not None else 2)
            plan.append(("send", sid, color, nxt, oz, ox, half))

    for color in (1, 0):
        sid = push("y", 0.0, (color, 0, 0, None), 1)
        plan.append(("send", sid, color, "y", 0, 0, None))
    count = {}
    parts = {}
    while heap:
        now, sq, link, key = heapq.heappop(heap)
        color, oz, ox, half = key
        first = "x" if color == 0 else "z"
        plan.append(("recv", sq - 1))
        size = {"x": NX, "z": NZ, "y": 2}[link[0]]
        whole = True
        if half is not None:
            spot = (color, oz % NZ, ox % NX)
            parts[spot] = parts.get(spot, 0) + 1
            whole = parts[spot] == 2
            if whole and link[0] == first:
                second = "z" if color == 0 else "x"
                for sign in "+-":
                    step = 1 if sign == "+" else -1
                    n_oz = oz - step if second == "z" else oz
                    n_ox = ox - step if second == "x" else ox
                    sid = push(second + sign, now, (color, n_oz, n_ox, None), 2)
                    plan.append(("send", sid, color, second + sign, oz, ox, None))
        else:
            emit(now, color, link, oz, ox)
        if whole:
            spot = (color, oz % NZ)
            count[spot] = count.get(spot, 0) + 1
            if count[spot] == NX:
                plan.append(("product", color, oz % NZ))
    return plan, seq[0], max(links.free.values())


COLOURS = (
    (0, 256, False, "x"),
    (256, 512, True, "z"),
    (512, 640, True, "z"),
    (640, 1024, True, "x"),
)
CHUNKS = (4, 3, 5, 2, 6, 1, 7, 0)
CHUNK_US = 1.3
TASK_US = 0.12
ADD_RATE = 1e6


def ring(first, stage):
    axis = first if stage == 1 else ("x" if first == "z" else "z")
    return axis, {"x": NX, "z": NZ}[axis]


def reduce_plan(colours):
    links = Links()
    needs = {}
    for color, (lo, hi, paired, first) in enumerate(colours):
        for stage in (1, 2):
            axis, n = ring(first, stage)
            for inst in CHUNKS if stage == 1 and first == "x" else (0,):
                for flow in (-1, 1):
                    for k in range(n // 2, 0, -1):
                        there = (flow * k) % n
                        if stage == 1:
                            dep = [("chunk", color, there if first == "z" else inst)]
                        else:
                            dep = [("q", color, 1, there if first == "x" else 0)]
                        if k < n // 2:
                            dep.append(("got", color, stage, flow, inst, k + 1))
                        needs["s", color, stage, flow, inst, k] = dep
                dep = [("got", color, stage, flow, inst, 1) for flow in (-1, 1)]
                dep.append(("chunk", color, 0 if first == "z" else inst) if stage == 1 else ("q", color, 1, 0))
                needs["q", color, stage, inst] = dep
        if not paired:
            needs["y", color] = [("q", color, 2, 0)]
            needs["out", color] = [("goty", color)]
    done = set()
    plan = []
    heap = []
    seq = 0

    def post(t, event):
        nonlocal seq
        seq += 1
        heapq.heappush(heap, (t, seq, event))

    queue = []
    for color, (lo, hi, paired, _) in enumerate(colours):
        ready = links.send("y", 0.0, 512 * (hi - lo) * 2) if paired else 0.0
        queue += [(ready, ("chunk", color, oz)) for oz in CHUNKS]
    post(*queue.pop(0))
    sids = {}
    core = 0.0
    while heap:
        t, _, event = heapq.heappop(heap)
        core = max(core, t)
        done.add(event)
        if event[0] == "chunk":
            plan.append(event)
            lo, hi = colours[event[1]][:2]
            core += CHUNK_US * (hi - lo) / 1024
            if queue:
                ready, nxt = queue.pop(0)
                post(max(core, ready), nxt)
        moved = True
        while moved:
            moved = False
            for task in list(needs):
                if not all(d in done for d in needs[task]):
                    continue
                del needs[task]
                plan.append(task)
                moved = True
                lo, hi, paired, first = colours[task[1]]
                rows = 32 if paired else 64
                core += TASK_US
                if task[0] == "s":
                    _, color, stage, flow, inst, k = task
                    axis, n = ring(first, stage)
                    nbytes = (1 if k == n // 2 else 2) * rows * (hi - lo) * 2
                    if stage == 1 and first == "z":
                        nbytes *= NX
                    if k < n // 2:
                        core += nbytes / ADD_RATE
                    post(links.send((axis, flow), core, nbytes), ("got",) + task[1:])
                    sids[task] = len(sids)
                elif task[0] == "y":
                    post(links.send("y", core, 64 * (hi - lo) * 2), ("goty", task[1]))
                    sids[task] = len(sids)
                elif task[0] == "q":
                    done.add(task)
    return plan, sids, core


def send(src, dst, ssem, rsem, dev):
    c = pltpu.make_async_remote_copy(
        src_ref=src, dst_ref=dst, send_sem=ssem, recv_sem=rsem, device_id=dev, device_id_type=MESH
    )
    c.start()
    return c


def tdot(a, b):
    return lax.dot_general(a, b, (((0,), (0,)), ((), ())), preferred_element_type=F32)


def layer_kernel(
    gplan, rplan, sids, scale,
    code_ref, bound_ref, rv_ref, gb_ref, cs_ref, tok_hbm, q_hbm, k_hbm, gate_hbm, tgt_hbm,
    gated_hbm, out_ref,
    tok, q, k, gate, tgt, w_own, factor, wa, wb, acc, v, wts, qd, kd, go, ga, gv, hold, rates,
    packed, xbuf, pref, tbuf, ybuf, zbuf, rbuf, obuf, ebuf, sums, got, inv, inn,
    tok_t, tp, gp,
    lsem, gs, gr, s1, r1, s2, r2, s3, r3, s4, r4, ps, pr, rs, rr, ts, tr, us, ur, hs, hr,
    *lots,
):
    x, y, z, wt = place()
    j = y * NZ + z
    rows = [lax.rem(x + n, NX) for n in range(1, NX)]
    cols = [lax.rem(j + n, NY * NZ) for n in range(1, NY * NZ)]
    row_dev = [at(p, y, z, wt) for p in rows]
    col_dev = [at(x, lax.div(p, NZ), lax.rem(p, NZ), wt) for p in cols]
    side_dev = [at(x, y, z, lax.rem(wt + n, 4)) for n in range(1, 4)]
    peers = {
        "x+": at(lax.rem(x + 1, NX), y, z, wt),
        "x-": at(lax.rem(x + NX - 1, NX), y, z, wt),
        "z+": at(x, y, lax.rem(z + 1, NZ), wt),
        "z-": at(x, y, lax.rem(z + NZ - 1, NZ), wt),
        "y": at(x, 1 - y, z, wt),
    }
    barrier = pltpu.get_barrier_semaphore()
    partners = row_dev + col_dev + side_dev
    for peer in partners:
        pl.semaphore_signal(barrier, inc=1, device_id=peer, device_id_type=MESH)
    loads = [
        pltpu.make_async_copy(a, b, lsem.at[n])
        for n, (a, b) in enumerate(
            [(tok_hbm, tok), (q_hbm, q), (k_hbm, k), (gate_hbm, gate), (tgt_hbm, tgt)]
        )
    ]
    for c in (1, 2, 0, 3, 4):
        loads[c].start()

    squash = jax.nn.sigmoid(rv_ref[...])
    raw = 1.2 * squash - 0.1
    w_own[...] = (
        cs_ref[...] * (gb_ref[...].astype(F32) + jnp.clip(raw, 0.0, 1.0))
    ).astype(BF)
    factor[...] = cs_ref[...] * jnp.where(
        (raw > 0.0) & (raw < 1.0), 1.2 * squash * (1.0 - squash), 0.0
    )
    pl.semaphore_wait(barrier, len(partners))

    def rate_of(h, shape):
        return jnp.exp2(jnp.full(shape, -code_ref[h].astype(F32), F32))

    mult = [1.0 - 0.5 * bound_ref[c].astype(F32) for c in range(2)]

    def head_tables(h):
        lo = h * HEAD
        rate = rate_of(h, (1, HEAD))
        row = lax.broadcasted_iota(jnp.int32, (GROUP, HEAD), 0).astype(F32)
        qdec = jnp.exp(-(row * rate))
        kdec = jnp.exp(-((GROUP - row) * rate))
        i = lax.broadcasted_iota(jnp.int32, (GROUP, GROUP), 0)
        o = lax.broadcasted_iota(jnp.int32, (GROUP, GROUP), 1)
        gap = (i - o).astype(F32)
        causal = jnp.where(
            gap >= 0.0, jnp.exp(-(jnp.maximum(gap, 0.0) * rate_of(h, (1, GROUP)))), 0.0
        )
        rates[h * 8 : h * 8 + 8] = jnp.broadcast_to(jnp.exp(-GROUP * rate)[None], (8, 1, HEAD))
        for c in range(2):
            r = slice(c * GROUP, c * GROUP + GROUP)
            qh = q[r, lo : lo + HEAD]
            kh = k[r, lo : lo + HEAD]
            score = lax.dot_general(qh, kh, (((1,), (1,)), ((), ())), preferred_element_type=F32)
            wts[c, h] = (score * causal).astype(BF)
            qd[r, lo : lo + HEAD] = (qh.astype(F32) * qdec).astype(BF)
            kd[r, lo : lo + HEAD] = (kh.astype(F32) * kdec).astype(BF)

    def open_gates():
        go[...] = jax.nn.sigmoid(gate[...].astype(F32))

    def turn_tokens(n):
        tok_t[n * 512 : n * 512 + 512] = tok[:, n * 512 : n * 512 + 512].T

    fillers = [functools.partial(head_tables, h) for h in range(8)] + [open_gates]
    fillers += [functools.partial(turn_tokens, n) for n in range(8)]
    def filler():
        if len(fillers) == 17:
            for c in (0, 1, 2, 3):
                loads[c].wait()
        if fillers:
            fillers.pop(0)()

    buf = (wa, wb)
    copies = {}
    for n, op in enumerate(gplan):
        if op[0] == "send":
            _, sid, color, link, oz, ox, half = op
            w = buf[color]
            if link == "y":
                lo, hi = LANES[color]
                src = w_own.at[:, lo:hi]
                dst = w.at[y, z, x]
            else:
                zz = lax.rem(z + (oz + 2 * NZ), NZ)
                xx = lax.rem(x + (ox + 2 * NX), NX)
                dst = w.at[:, zz, xx] if half is None else w.at[half, zz, xx]
                src = dst
            copies[sid] = send(src, dst, gs.at[sid], gr.at[sid], peers[link])
            if len(copies) == 2:
                wa[y, z, x] = w_own[:, :SPLIT]
                wb[y, z, x] = w_own[:, SPLIT:]
                acc[...] = jnp.zeros_like(acc)
        elif op[0] == "recv":
            copies[op[1]].wait_recv()
        else:
            _, color, oz = op
            zz = lax.rem(z + oz, NZ)
            lo, hi = LANES[color]
            w = buf[color]

            @pl.loop(0, 4)
            def _(i, zz=zz, lo=lo, hi=hi, w=w):
                r = pl.ds(pl.multiple_of(i * 128, 128), 128)
                t0 = tok[r, pl.ds(pl.multiple_of(zz * 256, 256), 256)]
                t1 = tok[r, pl.ds(pl.multiple_of(zz * 256 + 2048, 256), 256)]
                acc[r, lo:hi] += jnp.dot(
                    t0, w[0, zz].reshape(256, hi - lo), preferred_element_type=F32
                ) + jnp.dot(t1, w[1, zz].reshape(256, hi - lo), preferred_element_type=F32)
        if n >= 12 and n % 8 == 4 or n == 14:
            filler()
    while fillers:
        filler()

    core = lax.rem(wt, 2)
    twin = at(x, y, z, wt + 1 - 2 * core)
    trade = []

    def trade_tokens(first, last):
        for n in range(first, last):
            r = pl.ds(pl.multiple_of(core * 1024 + n * 128, 128), 128)
            src = tok_t.at[pl.ds(pl.multiple_of((1 - y) * 2048 + core * 1024 + n * 128, 128), 128)]
            trade.append(send(src, tp.at[r], ts.at[n], tr.at[n], peers["y"]))

    trade_tokens(0, 2)

    def scan(f, reverse, meanwhile, later):
        one = [
            send(packed.at[f, p], xbuf.at[f, x], s1.at[f, n], r1.at[f, n], d)
            for n, (p, d) in enumerate(zip(rows, row_dev))
        ]
        xbuf[f, x] = packed[f, x]
        meanwhile()
        rate = rates[pl.ds(x * 16, 16)]
        rate = rate * rate
        rate1 = rates[x * 16 + j]
        rate1 = rate1 * rate1
        rate4 = (rate1 * rate1) * (rate1 * rate1)
        for c in one:
            c.wait_recv()
        order = list(reversed(range(NX))) if reverse else list(range(NX))
        total = jnp.zeros((16, 16, 128), F32)
        m_all = jnp.ones((16, 128), F32)
        mults = []
        for i in order:
            pref[i] = total
            mults.append(m_all)
            m = xbuf[f, i, 16].astype(F32)
            total = (rate * m[None]) * total + xbuf[f, i, pl.ds(0, 16)].astype(F32)
            m_all = m_all * m
        tbuf[f, :, 0] = total.astype(BF)
        tbuf[f, :, 1] = jnp.broadcast_to(m_all.astype(BF)[None], (16, 16, 128))
        two = [
            send(tbuf.at[f, p], ybuf.at[f, j], s2.at[f, n], r2.at[f, n], d)
            for n, (p, d) in enumerate(zip(cols, col_dev))
        ]
        ybuf[f, j] = tbuf[f, j]
        for c in two:
            c.wait_recv()
        state = jnp.zeros((16, 128), F32)
        span = NY * NZ
        for i in reversed(range(span)) if reverse else range(span):
            zbuf[f, i] = state.astype(BF)
            state = (rate4 * ybuf[f, i, 1].astype(F32)) * state + ybuf[f, i, 0].astype(F32)
        three = [
            send(zbuf.at[f, p], rbuf.at[f, j], s3.at[f, n], r3.at[f, n], d)
            for n, (p, d) in enumerate(zip(cols, col_dev))
        ]
        rbuf[f, j] = zbuf[f, j]
        for c in three:
            c.wait_recv()
        later()
        entering = rbuf[f].astype(F32)
        grow = jnp.ones((16, 1, 128), F32)
        for n, i in enumerate(order):
            obuf[f, i] = (pref[i] + (grow * mults[n][None]) * entering).astype(BF)
            grow = grow * rate
        four = [
            send(obuf.at[f, p], ebuf.at[f, x], s4.at[f, n], r4.at[f, n], d)
            for n, (p, d) in enumerate(zip(rows, row_dev))
        ]
        ebuf[f, x] = obuf[f, x]
        for c in four:
            c.wait_recv()
        return one + two + three + four

    def pack(f, h, part):
        packed[f, h // 2, (h % 2) * 8 : (h % 2) * 8 + 8] = part.astype(BF).reshape(8, 16, 128)

    def entered(f, h):
        return ebuf[f, h // 2, (h % 2) * 8 : (h % 2) * 8 + 8].reshape(HEAD, HEAD).astype(F32)

    def span_of(c, h):
        return slice(c * GROUP, c * GROUP + GROUP), slice(h * HEAD, h * HEAD + HEAD)

    for f in range(2):
        for n in range(NX):
            packed[f, n, 16] = jnp.full((16, 128), mult[0] * mult[1], F32).astype(BF)
    for h in range(8):
        fade = rates[h * 8]
        for c in range(2):
            r, l = span_of(c, h)
            v[r, l] = acc[r, l].astype(BF)
        u0 = tdot(kd[span_of(0, h)], v[span_of(0, h)])
        u1 = tdot(kd[span_of(1, h)], v[span_of(1, h)])
        hold[h] = u0
        pack(0, h, (fade * mult[1]) * u0 + u1)

    def intra():
        for h in range(8):
            for c in range(2):
                r, l = span_of(c, h)
                acc[r, l] = jnp.dot(wts[c, h], v[r, l], preferred_element_type=F32)

    scans = scan(0, False, intra, lambda: trade_tokens(2, 8))

    sums[12:16] = jnp.zeros((4, 128), F32)
    loads[4].wait()
    for c in range(2):
        square = jnp.zeros((GROUP, HEAD), F32)
        opened = jnp.zeros((GROUP, HEAD), F32)
        cross = jnp.zeros((GROUP, HEAD), F32)
        for h in range(8):
            r, l = span_of(c, h)
            fade = rates[h * 8]
            if c == 0:
                state = mult[0] * entered(0, h)
            else:
                state = mult[1] * hold[h] + (fade * (mult[0] * mult[1])) * entered(0, h)
            attn = acc[r, l] + jnp.dot(qd[r, l], state.astype(BF), preferred_element_type=F32)
            acc[r, l] = attn
            gated = attn * go[r, l]
            square = square + attn * attn
            opened = opened + gated * gated
            cross = cross + gated * tgt[r, l].astype(F32)
        for kind, part in enumerate((square, opened, cross)):
            for b in range(2):
                block = part[b * 128 : b * 128 + 128].T
                n = kind * 4 + c * 2 + b
                sums[n : n + 1] = jnp.sum(block, axis=0, keepdims=True)
    side = [
        send(sums, got.at[wt], ps.at[n], pr.at[n], d) for n, d in enumerate(side_dev)
    ]
    got[wt] = sums[...]
    for c in side:
        c.wait_recv()
    total = (got[0] + got[1]) + (got[2] + got[3])
    width = HEADS * HEAD
    inv_row = 1.0 / jnp.sqrt(total[0:4] / width + epsilon)
    inner_row = (scale * (total[4:8] * inv_row - total[8:12]) * inv_row) / width
    for n in range(4):
        r = slice(n * 128, n * 128 + 128)
        inv[r] = jnp.broadcast_to(inv_row[n : n + 1], (128, 128)).T
        inn[r] = jnp.broadcast_to(inner_row[n : n + 1], (128, 128)).T
    out_buf = q
    for h in range(8):
        fade = rates[h * 8]
        for c in range(2):
            r, l = span_of(c, h)
            normed = acc[r, l] * inv[r]
            gate_open = go[r, l]
            gated = normed * gate_open
            out_buf[r, l] = gated.astype(BF)
            grad_normed = ((gated - tgt[r, l].astype(F32)) * scale) * gate_open
            ga[r, l] = ((grad_normed - normed * inn[r]) * inv[r]).astype(BF)
        c0 = tdot(qd[span_of(0, h)], ga[span_of(0, h)])
        c1 = tdot(qd[span_of(1, h)], ga[span_of(1, h)])
        hold[h] = c1
        pack(1, h, mult[0] * c0 + (fade * (mult[0] * mult[1])) * c1)
    store = pltpu.make_async_copy(out_buf, gated_hbm, lsem.at[5])
    store.start()

    def back_intra():
        for h in range(8):
            for c in range(2):
                r, l = span_of(c, h)
                acc[r, l] = tdot(wts[c, h], ga[r, l])
        for n, c in enumerate(trade):
            c.wait_recv()
            r = pl.ds(pl.multiple_of(core * 1024 + n * 128, 128), 128)
            share.append(send(tp.at[r], tp.at[r], us.at[n], ur.at[n], twin))

    share = []
    scans += scan(1, True, back_intra, lambda: None)
    grads = {}

    def value_grads(h):
        fade = rates[h * 8]
        for c in range(2):
            r, l = span_of(c, h)
            state = entered(1, h)
            if c == 0:
                state = mult[1] * hold[h] + (fade * mult[1]) * state
            gv[r, l] = (
                acc[r, l] + jnp.dot(kd[r, l], state.astype(BF), preferred_element_type=F32)
            ).astype(BF)

    for color, (lo, hi, paired, _) in sorted(enumerate(COLOURS), key=lambda e: not e[1][2]):
        for h in range(lo // HEAD, hi // HEAD):
            value_grads(h)
        if paired:
            grads[color] = send(
                gv.at[:, lo:hi], gp.at[:, lo:hi], hs.at[color], hr.at[color], peers["y"]
            )

    bufs = [lots[n : n + 7] for n in range(0, len(lots), 7)]
    moves = {}
    arrived = set()

    def slot(color, stage, flow, inst, n):
        r = bufs[color][stage]
        f = 0 if flow < 0 else 1
        return r.at[f, inst, n] if stage == 1 else r.at[f, n]

    def own(color, stage, inst, there):
        if COLOURS[color][3] == "z":
            if stage == 2:
                return bufs[color][3].at[lax.rem(x + there, NX)]
            return bufs[color][0].at[lax.rem(z + there, NZ)]
        if stage == 2:
            return bufs[color][3].at[there]
        return bufs[color][0].at[lax.rem(z + inst, NZ), lax.rem(x + there, NX)]

    for op in rplan:
        color = op[1]
        lo, hi, paired, first = COLOURS[color]
        if op[0] == "chunk":
            zz = lax.rem(z + op[2], NZ)
            part = bufs[color][0]
            if paired:
                if not arrived:
                    for c in share:
                        c.wait_recv()
                if color not in arrived:
                    grads[color].wait_recv()
                    arrived.add(color)

                mine = tok_t[pl.ds(pl.multiple_of(y * 2048 + zz * 256, 256), 256)]
                other = tp[pl.ds(pl.multiple_of(zz * 256, 256), 256)]
                r = jnp.dot(mine, gv[:, lo:hi], preferred_element_type=F32)
                r = r + jnp.dot(other, gp[:, lo:hi], preferred_element_type=F32)
                part[zz] = r.astype(BF).reshape(NX, 2, 32, hi - lo)
            else:
                for yy in range(2):
                    mine = tok_t[pl.ds(pl.multiple_of(yy * 2048 + zz * 256, 256), 256)]
                    r = jnp.dot(mine, gv[:, lo:hi], preferred_element_type=F32).astype(BF)
                    for u in range(NX):
                        part[zz, u, yy] = r[u * 64 : u * 64 + 64]
        elif op[0] == "s":
            _, color, stage, flow, inst, n = op
            axis, size = ring(first, stage)
            half = 0 if flow < 0 else 1
            rest = 1 - half
            if stage == 1 and first == "z":
                half, rest = (slice(None), half), (slice(None), rest)
            p = own(color, stage, inst, (flow * n) % size)
            if n == size // 2:
                src = p.at[half]
                dst = slot(color, stage, flow, inst, n - 1).at[half]
            else:
                moves["s", color, stage, flow, inst, n + 1].wait_recv()
                src = slot(color, stage, flow, inst, n)
                dst = slot(color, stage, flow, inst, n - 1)
                if n == size // 2 - 1:
                    src[half] = (src[half].astype(F32) + p[half].astype(F32)).astype(BF)
                    src[rest] = p[rest]
                else:
                    src[...] = (src[...].astype(F32) + p[...].astype(F32)).astype(BF)
            sid = sids[op]
            link = axis + ("+" if flow > 0 else "-")
            moves[op] = send(src, dst, rs.at[sid], rr.at[sid], peers[link])
        elif op[0] == "q":
            _, color, stage, inst = op
            for flow in (-1, 1):
                moves["s", color, stage, flow, inst, 1].wait_recv()
            low = slot(color, stage, -1, inst, 0)
            high = slot(color, stage, 1, inst, 0)
            p = own(color, stage, inst, 0)
            total = low[...].astype(F32) + high[...].astype(F32) + p[...].astype(F32)
            if stage == 1 and first == "z":
                bufs[color][3][...] = total.astype(BF)
            elif stage == 1:
                bufs[color][3][inst] = total.astype(BF)
            elif paired:
                out_ref[:, lo:hi] = factor[:, lo:hi] * total.reshape(64, hi - lo)
            else:
                bufs[color][4][...] = total
        elif op[0] == "y":
            ysend, yrecv = bufs[color][5:7]
            ysend[...] = bufs[color][4][1 - y].astype(BF)
            sid = sids[op]
            moves[op] = send(ysend, yrecv, rs.at[sid], rr.at[sid], peers["y"])
        else:
            moves["y", color].wait_recv()
            out_ref[:, lo:hi] = factor[:, lo:hi] * (
                bufs[color][4][y] + bufs[color][6][...].astype(F32)
            )
    store.wait()
    for c in list(copies.values()) + scans + side + trade + share:
        c.wait_send()
    for c in list(grads.values()) + list(moves.values()):
        c.wait_send()


def on_device(
    tokens, round_var, grid_base, col_scale, queries, keys, gates, target, decay_code, boundary
):
    gplan, gn, _ = gather_plan()
    rplan, sids, _ = reduce_plan(COLOURS)
    rn = len(sids)
    scale = loss_weight / math.sqrt(tokens.shape[0] * lax.axis_size("ctx"))
    a, b = SPLIT, 1024 - SPLIT
    vm = pl.BlockSpec(memory_space=pltpu.VMEM)
    sm = pl.BlockSpec(memory_space=pltpu.SMEM)
    hbm = pl.BlockSpec(memory_space=pl.ANY)
    V = pltpu.VMEM
    D = pltpu.SemaphoreType.DMA
    scratch = [
        V((512, 4096), BF),
        V((512, 1024), BF), V((512, 1024), BF), V((512, 1024), BF), V((512, 1024), BF),
        V((64, 1024), BF), V((64, 1024), F32),
        V((NY, NZ, NX, 64, a), BF), V((NY, NZ, NX, 64, b), BF),
        V((512, 1024), F32), V((512, 1024), BF),
        V((2, 8, GROUP, GROUP), BF), V((512, 1024), BF), V((512, 1024), BF),
        V((512, 1024), F32), V((512, 1024), BF), V((512, 1024), BF),
        V((8, HEAD, HEAD), F32), V((64, 1, 128), F32),
        V((2, NX, 17, 16, 128), BF), V((2, NX, 17, 16, 128), BF),
        V((NX, 16, 16, 128), F32),
        V((2, 16, 2, 16, 128), BF), V((2, 16, 2, 16, 128), BF),
        V((2, 16, 16, 128), BF), V((2, 16, 16, 128), BF),
        V((2, NX, 16, 16, 128), BF), V((2, NX, 16, 16, 128), BF),
        V((16, 128), F32), V((4, 16, 128), F32),
        V((512, 128), F32), V((512, 128), F32),
        V((4096, 512), BF), V((2048, 512), BF), V((512, 1024), BF),
        D((6,)), D((gn,)), D((gn,)),
        D((2, 3)), D((2, 3)), D((2, 15)), D((2, 15)), D((2, 15)), D((2, 15)), D((2, 3)), D((2, 3)),
        D((3,)), D((3,)), D((rn,)), D((rn,)),
        D((8,)), D((8,)), D((8,)), D((8,)), D((len(COLOURS),)), D((len(COLOURS),)),
    ]
    for lo, hi, paired, first in COLOURS:
        r, w = 32 if paired else 64, hi - lo
        n1, n2 = (NX, NZ) if first == "z" else (NZ, NX)
        f = 8 if paired else 64
        lot = (2, 1, n2 // 2, NX, 2, r, w) if first == "z" else (2, n1, n2 // 2, 2, r, w)
        scratch += [
            V((NZ, NX, 2, r, w), BF), V(lot, BF),
            V((2, n1 // 2, 2, r, w), BF), V((n1, 2, r, w), BF),
            V((2, f, w), F32), V((f, w), BF), V((f, w), BF),
        ]
    return pl.pallas_call(
        functools.partial(layer_kernel, gplan, rplan, sids, scale),
        out_shape=(
            jax.ShapeDtypeStruct((512, 1024), BF),
            jax.ShapeDtypeStruct((64, 1024), F32),
        ),
        in_specs=[sm, sm, vm, vm, vm, hbm, hbm, hbm, hbm, hbm],
        out_specs=(hbm, vm),
        scratch_shapes=scratch,
        compiler_params=pltpu.CompilerParams(
            collective_id=0, has_side_effects=True, vmem_limit_bytes=62 * 2**20
        ),
        name="layer_step",
    )(
        decay_code, boundary, round_var, grid_base, col_scale.reshape(1, -1), tokens, queries,
        keys, gates, target,
    )


def solution(mesh):
    placed = (
        P("ctx", None),
        P("ctx", "wt"),
        P("ctx", "wt"),
        P("wt"),
        P("ctx", "wt"),
        P("ctx", "wt"),
        P("ctx", "wt"),
        P("ctx", "wt"),
        P("wt"),
        P("ctx"),
    )
    return jax.shard_map(
        on_device,
        mesh=mesh,
        in_specs=placed,
        out_specs=(P("ctx", "wt"), P("ctx", "wt")),
        check_vma=False,
    )
```
